512 devices in a mesh: dp: 128 (over y, z, core), mp: 4 (over x).
Axes of the slice: x: 4, y: 4, z: 16, core: 2. Of those that a mesh axis runs over, the one named last changes fastest.
Arguments:
- embeddings: bfloat16 [32768, 768], P('dp'), may hold values from -8192 to 8192
- cluster_ids: int32 [32768], P('dp'), may hold values from 0 to 511, as said below
Outputs:
- scores: float32 [32768], P('dp')
The draws below stay inside these ranges and needn't reach their ends.
Inputs may be any that keep to these rules, and one draw needn't show every extreme that they name: `cluster_ids`: the owner of cluster c is the index c // 4 of dp. Of the 256 rows of one index of dp, at most 4 lie in the clusters of one owner, and some owner gets exactly 4 rows from every index of dp.
All inputs are finite; a program needn't handle non-finite values.
Results may differ from the reference program's by a relative error of at most 0.0018.
Values may be sent and summed in bfloat16 or wider, within the bound.
A program may use at most 64 MiB of HBM per device.

```python
import math
import jax
import jax.numpy as jnp
from jax import lax

D = 768
ROWS_DEV = 256
CPO = 4
PAIR = 4
SLOTS = 512
BLOCKS = 512
RQ = 64
N_DP = 128


def layout_draw(key):
    base_key = jax.random.fold_in(key, 11)
    slot_total = 2 * ROWS_DEV
    owner_count = slot_total // PAIR
    groups = max(ROWS_DEV // 16, 1)
    levels = jax.random.randint(jax.random.fold_in(base_key, 1), (owner_count,), 0, 4) * (slot_total // 2)
    hottest = jax.random.randint(jax.random.fold_in(base_key, 2), (), 0, owner_count)
    owner_range = jnp.arange(owner_count)
    forced = (owner_range == hottest) | (owner_range == 0) | (owner_range == owner_count - 1)
    levels = jnp.where(forced, 8 * slot_total, levels)
    slot_owner = jnp.arange(slot_total) // PAIR

    def one_source(source):
        source_key = jax.random.fold_in(base_key, 100 + source)
        shuffled = jax.random.permutation(jax.random.fold_in(source_key, 1), slot_total)
        priority = (levels[slot_owner] + shuffled) * slot_total + jnp.arange(slot_total)
        chosen = jnp.argsort(-priority, stable=True)[:ROWS_DEV]
        mixing = jax.random.permutation(jax.random.fold_in(source_key, 2), ROWS_DEV)
        picked = chosen[mixing]
        owners = picked // PAIR
        within = jax.random.randint(jax.random.fold_in(source_key, 3), (ROWS_DEV,), 0, CPO)
        first_slot = picked % PAIR == 0
        within = jnp.where(first_slot & (owners == 0), 0, within)
        within = jnp.where(first_slot & (owners == owner_count - 1), CPO - 1, within)
        group_ids = jax.random.randint(jax.random.fold_in(source_key, 4), (ROWS_DEV,), 0, groups)
        return (owners * CPO + within, group_ids)
    cluster_ids, group_ids = jax.vmap(one_source)(jnp.arange(owner_count))
    return (cluster_ids.reshape(-1).astype(jnp.int32), group_ids.reshape(-1).astype(jnp.int32))


def draw_cluster_ids(key, part):
    cluster_ids, group_ids = layout_draw(key)
    return cluster_ids


def draw_embeddings(key, part):
    cluster_ids, group_ids = layout_draw(key)
    row_total = cluster_ids.shape[0]
    groups = max(ROWS_DEV // 16, 1)
    float_key = jax.random.fold_in(key, 29)
    shared_key = jax.random.fold_in(key, 31)
    direction_key = jax.random.fold_in(key, 37)
    direction_count = 32
    group_codes = cluster_ids * groups + group_ids
    own_part = jax.random.truncated_normal(jax.random.fold_in(float_key, 1), -4.0, 4.0, (row_total, D), jnp.float32)
    directions = jax.random.truncated_normal(direction_key, -4.0, 4.0, (direction_count, D), jnp.float32)

    def group_vector(code):
        return jax.random.truncated_normal(jax.random.fold_in(shared_key, code), -4.0, 4.0, (D,), jnp.float32)
    shared_part = jax.vmap(group_vector)(group_codes)
    own_weight = jnp.exp(jax.random.uniform(jax.random.fold_in(float_key, 2), (row_total, 1), jnp.float32, math.log(0.15), 0.0))
    is_copy = (jax.random.randint(jax.random.fold_in(float_key, 3), (row_total, 1), 0, 10) < 7).astype(jnp.float32)
    row_scale = jnp.exp(jax.random.uniform(jax.random.fold_in(float_key, 4), (row_total, 1), jnp.float32, 0.0, math.log(10.0)))
    col_scale = jnp.exp(jax.random.uniform(jax.random.fold_in(float_key, 5), (D,), jnp.float32, 0.0, math.log(3.0)))
    blocks_share = max(BLOCKS // D, 1)
    amplitude = math.sqrt(2.0 * BLOCKS / blocks_share)
    block_of_row = jnp.arange(row_total) // RQ
    spike_cols = jax.random.permutation(jax.random.fold_in(float_key, 6), D)[block_of_row % D]
    spike_value = jax.random.truncated_normal(jax.random.fold_in(float_key, 7), -4.0, 4.0, (row_total,), jnp.float32) * amplitude
    direction_index = jax.random.randint(jax.random.fold_in(float_key, 8), (row_total, 4), 0, direction_count)
    direction_weight = jax.random.uniform(jax.random.fold_in(float_key, 9), (row_total, 4), jnp.float32, -1.0, 1.0)
    correlated = direction_weight[:, 0:1] * directions[direction_index[:, 0]]
    correlated = correlated + direction_weight[:, 1:2] * directions[direction_index[:, 1]]
    correlated = correlated + direction_weight[:, 2:3] * directions[direction_index[:, 2]]
    correlated = correlated + direction_weight[:, 3:4] * directions[direction_index[:, 3]]
    mixed = own_weight * own_part + is_copy * shared_part + correlated
    mixed = mixed.at[jnp.arange(row_total), spike_cols].add(spike_value)
    values = row_scale * col_scale[None, :] * mixed
    return values.astype(jnp.bfloat16)


def setup_inputs(seed: int = 0) -> dict:
    keys = jax.random.split(jax.random.key(seed), 3)
    return {
        "embeddings": draw_embeddings(jax.random.fold_in(keys[2], 71), 0),
        "cluster_ids": draw_cluster_ids(jax.random.fold_in(keys[2], 71), 0),
    }


def normalize_rows(values):
    widened = values.astype(jnp.float32)
    square_sum = lax.optimization_barrier(jnp.sum(widened * widened, axis=1, keepdims=True))
    inverse_norm = lax.rsqrt(square_sum + 1e-06)
    return (widened * inverse_norm).astype(jnp.bfloat16)

def reference(embeddings, cluster_ids):
    row_total = embeddings.shape[0]
    identity = jnp.eye(D, dtype=jnp.float32)
    moments = lax.dot_general(embeddings.astype(jnp.float32), embeddings.astype(jnp.float32), (((0,), (0,)), ((), ())), preferred_element_type=jnp.float32)
    chol_factor = jnp.linalg.cholesky(moments / row_total + 0.001 * identity)
    whitening = jax.scipy.linalg.solve_triangular(chol_factor, identity, lower=True).astype(jnp.bfloat16)
    whitened = lax.dot_general(embeddings.astype(jnp.float32), whitening.astype(jnp.float32), (((1,), (1,)), ((), ())), preferred_element_type=jnp.float32).astype(jnp.bfloat16)
    unit = normalize_rows(whitened)
    owner_ids = (cluster_ids // CPO).astype(jnp.int32)
    sort_order = jnp.argsort(owner_ids, stable=True).astype(jnp.int32)
    counts = jax.ops.segment_sum(jnp.ones((row_total,), jnp.int32), owner_ids, num_segments=N_DP).astype(jnp.int32)
    starts = (jnp.cumsum(counts) - counts).astype(jnp.int32)
    capacity = SLOTS
    unit_sorted = jnp.concatenate([unit[sort_order], jnp.zeros((capacity, D), jnp.bfloat16)], axis=0)
    ids_sorted = jnp.concatenate([cluster_ids[sort_order], jnp.full((capacity,), -1, jnp.int32)], axis=0)
    local_pos = jnp.arange(capacity, dtype=jnp.int32)

    def per_owner(owner_index):
        first_row = starts[owner_index]
        key_units = lax.dynamic_slice_in_dim(unit_sorted, first_row, capacity, 0)
        key_ids = lax.dynamic_slice_in_dim(ids_sorted, first_row, capacity, 0)
        key_ids = jnp.where(local_pos < counts[owner_index], key_ids, -1)
        similarity = lax.dot_general(key_units.astype(jnp.float32), key_units.astype(jnp.float32), (((1,), (1,)), ((), ())), preferred_element_type=jnp.float32)
        same_cluster = (key_ids[:, None] == key_ids[None, :]) & (key_ids[:, None] >= 0) & (local_pos[:, None] != local_pos[None, :])
        return lax.optimization_barrier(jnp.max(jnp.where(same_cluster, similarity, -1.0), axis=1))
    owner_table = lax.map(per_owner, jnp.arange(N_DP, dtype=jnp.int32))
    owner_sorted = owner_ids[sort_order]
    position = (jnp.arange(row_total, dtype=jnp.int32) - starts[owner_sorted]).astype(jnp.int32)
    sorted_scores = owner_table[owner_sorted, position]
    return jnp.zeros((row_total,), jnp.float32).at[sort_order].set(sorted_scores)
```

```python
import functools

import jax
import jax.numpy as jnp
from jax import lax
from jax.experimental import pallas as pl
from jax.experimental.pallas import tpu as pltpu
from jax.sharding import PartitionSpec as P

CPO = 4
NX, NC, NY, NZ = 4, 2, 4, 16
BLK = 128
NB = 6
D = NB * BLK
MESH = pl.DeviceIdType.MESH
HIGH = lax.Precision.HIGHEST


def moments_kernel(x_ref, out_ref, part, got_c, half, got_y, quarter, got_z,
                   c_send, c_recv, y_send, y_recv, z_send, z_recv,
                   gz_send, gz_recv, a_send, a_recv, b_send, b_recv,
                   a2_send, a2_recv, b2_send, b2_recv, gc_send, gc_recv):
    m = lax.axis_index("mp")
    d = lax.axis_index("dp")
    c = lax.rem(d, 2)
    z = lax.rem(lax.div(d, 2), NZ)
    y = lax.div(d, 2 * NZ)

    def dev(yy, zz, cc, mm):
        return ((yy * NZ + zz) * 2 + cc, mm)

    sibling = dev(y, z, 1 - c, m)
    y_peers = [lax.rem(y + o, NY) for o in (2, 1, 3)]
    z_peers = [lax.rem(z + o, NZ) for o in (8, 7, 9, 6, 10, 5, 11, 4, 12, 3, 13, 2, 14, 1, 15)]
    x_peers = [lax.rem(m + o, NX) for o in (2, 1, 3)]
    barrier = pltpu.get_barrier_semaphore()
    everyone = ([sibling] + [dev(p, z, c, m) for p in y_peers]
                + [dev(y, p, c, m) for p in z_peers] + [dev(y, z, c, p) for p in x_peers])
    for peer in everyone:
        pl.semaphore_signal(barrier, inc=1, device_id=peer, device_id_type=MESH)

    for i in range(NB):
        j = lax.rem(i + m, NB)
        left = x_ref[:, i * BLK:(i + 1) * BLK]
        right = x_ref[:, pl.ds(pl.multiple_of(j * BLK, BLK), BLK)]
        prod = lax.dot_general(left, right, (((0,), (0,)), ((), ())),
                               preferred_element_type=jnp.float32)
        part[:, :, :, i, :] = prod.reshape(NC, NY, NZ, BLK)
    pl.semaphore_wait(barrier, len(everyone))

    def copy(src, dst, send, recv, device):
        return pltpu.make_async_remote_copy(
            src_ref=src, dst_ref=dst, send_sem=send, recv_sem=recv,
            device_id=device, device_id_type=MESH)

    cc = copy(part.at[1 - c], got_c, c_send, c_recv, sibling)
    cc.start()
    cc.wait_recv()
    half[...] = part[c] + got_c[...]
    sent_y = []
    for p in y_peers:
        cp = copy(half.at[p], got_y.at[y], y_send.at[p], y_recv.at[y], dev(p, z, c, m))
        cp.start()
        sent_y.append(cp)
    total = half[y]
    for p in y_peers:
        copy(half.at[p], got_y.at[p], y_send.at[p], y_recv.at[p], dev(p, z, c, m)).wait_recv()
        total = total + got_y[p]
    quarter[...] = total
    sent_z = []
    for p in z_peers:
        cp = copy(quarter.at[p], got_z.at[z], z_send.at[p], z_recv.at[z], dev(y, p, c, m))
        cp.start()
        sent_z.append(cp)
    row = quarter[z]
    for p in reversed(z_peers):
        copy(quarter.at[p], got_z.at[p], z_send.at[p], z_recv.at[p], dev(y, p, c, m)).wait_recv()
        row = row + got_z[p]
    out_ref[m, c, y, z] = row
    gz = []
    for p in z_peers:
        cp = copy(out_ref.at[m, c, y, z], out_ref.at[m, c, y, z], gz_send.at[p], gz_recv.at[z],
                  dev(y, p, c, m))
        cp.start()
        gz.append(cp)
    for p in reversed(z_peers):
        copy(out_ref.at[m, c, y, p], out_ref.at[m, c, y, p], gz_send.at[p], gz_recv.at[p],
             dev(y, p, c, m)).wait_recv()
    lo, hi = pl.ds(0, NZ // 2), pl.ds(NZ // 2, NZ // 2)
    ga = []
    for p in y_peers:
        cp = copy(out_ref.at[m, c, y, lo], out_ref.at[m, c, y, lo], a_send.at[p], a_recv.at[y],
                  dev(p, z, c, m))
        cp.start()
        ga.append(cp)
    for p in x_peers:
        cp = copy(out_ref.at[m, c, y, hi], out_ref.at[m, c, y, hi], b_send.at[p], b_recv.at[m],
                  dev(y, z, c, p))
        cp.start()
        ga.append(cp)
    for p in y_peers:
        copy(out_ref.at[m, c, p, lo], out_ref.at[m, c, p, lo], a_send.at[p], a_recv.at[p],
             dev(p, z, c, m)).wait_recv()
    for p in x_peers:
        cp = copy(out_ref.at[m, c, :, lo], out_ref.at[m, c, :, lo], a2_send.at[p], a2_recv.at[m],
                  dev(y, z, c, p))
        cp.start()
        ga.append(cp)
    for p in x_peers:
        copy(out_ref.at[p, c, y, hi], out_ref.at[p, c, y, hi], b_send.at[p], b_recv.at[p],
             dev(y, z, c, p)).wait_recv()
    for p in y_peers:
        cp = copy(out_ref.at[:, c, y, hi], out_ref.at[:, c, y, hi], b2_send.at[p], b2_recv.at[y],
                  dev(p, z, c, m))
        cp.start()
        ga.append(cp)
    for p in x_peers:
        copy(out_ref.at[p, c, :, lo], out_ref.at[p, c, :, lo], a2_send.at[p], a2_recv.at[p],
             dev(y, z, c, p)).wait_recv()
    for p in y_peers:
        copy(out_ref.at[:, c, p, hi], out_ref.at[:, c, p, hi], b2_send.at[p], b2_recv.at[p],
             dev(p, z, c, m)).wait_recv()
    gc = copy(out_ref.at[:, c], out_ref.at[:, c], gc_send, gc_recv, sibling)
    gc.start()
    copy(out_ref.at[:, 1 - c], out_ref.at[:, 1 - c], gc_send, gc_recv, sibling).wait_recv()
    cc.wait_send()
    for cp in sent_y + sent_z + gz + ga:
        cp.wait_send()
    gc.wait_send()


def summed_moments(x):
    f32 = jnp.float32
    dma = pltpu.SemaphoreType.DMA
    scratch = [
        pltpu.VMEM((NC, NY, NZ, NB, BLK), f32),
        pltpu.VMEM((NY, NZ, NB, BLK), f32),
        pltpu.VMEM((NY, NZ, NB, BLK), f32),
        pltpu.VMEM((NY, NZ, NB, BLK), f32),
        pltpu.VMEM((NZ, NB, BLK), f32),
        pltpu.VMEM((NZ, NB, BLK), f32),
        dma, dma, dma((NY,)), dma((NY,)), dma((NZ,)), dma((NZ,)),
        dma((NZ,)), dma((NZ,)), dma((NY,)), dma((NY,)), dma((NX,)), dma((NX,)),
        dma((NX,)), dma((NX,)), dma((NY,)), dma((NY,)), dma, dma,
    ]
    return pl.pallas_call(
        moments_kernel,
        out_shape=jax.ShapeDtypeStruct((NX, NC, NY, NZ, NB, BLK), f32),
        in_specs=[pl.BlockSpec(memory_space=pltpu.VMEM)],
        out_specs=pl.BlockSpec(memory_space=pltpu.VMEM),
        scratch_shapes=scratch,
        name="moments",
        compiler_params=pltpu.CompilerParams(collective_id=0, has_side_effects=True),
    )(x)


def lower_inverse(block):
    lane = lax.broadcasted_iota(jnp.int32, (8, BLK), 1)
    sub = lax.broadcasted_iota(jnp.int32, (8, BLK), 0)
    groups = BLK // 8
    wide = (8, BLK)
    scales = []
    for t in range(groups):
        own = block[t]
        base = 8 * t
        cols = [jnp.broadcast_to(own[:, base + q:base + q + 1], wide) for q in range(8)]
        piv = [[None] * 8 for _ in range(8)]
        for q in range(8):
            for r in range(q, 8):
                piv[q][r] = jnp.broadcast_to(cols[r][q:q + 1, :], wide)
        mult = [[None] * 8 for _ in range(8)]
        inv = [None] * 8
        scale = None
        for q in range(8):
            inv[q] = 1.0 / piv[q][q]
            for r in range(q + 1, 8):
                mult[q][r] = piv[q][r] * inv[q]
            for r in range(q + 1, 8):
                for s in range(r, 8):
                    piv[r][s] = piv[r][s] - mult[q][r] * piv[q][s]
            root = lax.rsqrt(piv[q][q])
            root = root * (1.5 - 0.5 * piv[q][q] * root * root)
            scale = root if scale is None else jnp.where(sub == q, root, scale)
        scales.append(scale)
        rows = []
        for q in range(8):
            row = jnp.broadcast_to(own[q:q + 1, :], wide)
            row = jnp.where(lane == base + q, inv[q], row * inv[q])
            rows.append(row)
            masked = jnp.where(sub > q, cols[q], 0.0)
            own = jnp.where((lane == base + q) & (sub > q), 0.0, own) - masked * row
            for r in range(q + 1, 8):
                cols[r] = cols[r] - masked * mult[q][r]
        block[t] = own
        for s in range(t + 1, groups):
            cur = block[s]
            coef = [jnp.broadcast_to(cur[:, base + q:base + q + 1], wide) for q in range(8)]
            for q in range(8):
                cur = jnp.where(lane == base + q, 0.0, cur) - coef[q] * rows[q]
                for r in range(q + 1, 8):
                    coef[r] = coef[r] - coef[q] * mult[q][r]
            block[s] = cur
    for t in range(groups):
        diff = lane - sub - 8 * t
        block[t] = scales[t] * jnp.where(diff < 0, block[t], jnp.where(diff == 0, 1.0, 0.0))
    return block


def tdot(a, b):
    return lax.dot_general(a, b, (((0,), (0,)), ((), ())), precision=HIGH,
                           preferred_element_type=jnp.float32)


def score_kernel(row_total, mom_ref, rows_ref, idr_ref, idc_ref, out_ref, work, diag, white):
    scale = 1.0 / row_total
    eye = jnp.where(lax.broadcasted_iota(jnp.int32, (BLK, BLK), 0)
                    == lax.broadcasted_iota(jnp.int32, (BLK, BLK), 1), 0.001, 0.0)

    def at(i, j):
        return (slice(i * BLK, (i + 1) * BLK), slice(j * BLK, (j + 1) * BLK))

    for i in range(NB):
        for g in range(4):
            j = i + g
            if j < NB:
                val = mom_ref[g, :, i, :] * scale
                work[at(i, j)] = val + eye if g == 0 else val
            elif g < 3:
                work[at(j - NB, i)] = (mom_ref[g, :, i, :] * scale).T

    @pl.loop(0, NB)
    def _(k):
        for kk in range(NB):
            @pl.when(k == kk)
            def _():
                diag[...] = work[at(kk, kk)]
        block = lower_inverse([diag[8 * t:8 * t + 8, :] for t in range(BLK // 8)])
        for t in range(BLK // 8):
            diag[8 * t:8 * t + 8, :] = block[t]
        for kk in range(NB):
            @pl.when(k == kk)
            def _():
                rk = slice(kk * BLK, (kk + 1) * BLK)
                inverse = diag[...]
                row = lax.dot_general(inverse, work[rk, :], (((1,), (0,)), ((), ())),
                                      precision=HIGH, preferred_element_type=jnp.float32)
                work[rk, :] = row
                work[at(kk, kk)] = inverse
                for i in range(kk + 1, NB):
                    ri = slice(i * BLK, (i + 1) * BLK)
                    left = work[at(kk, i)]
                    if kk:
                        work[ri, :kk * BLK] = work[ri, :kk * BLK] - tdot(left, work[rk, :kk * BLK])
                    work[at(i, kk)] = -tdot(left, inverse)
                    work[ri, i * BLK:] = work[ri, i * BLK:] - tdot(left, work[rk, i * BLK:])

    for k in range(NB):
        for j in range(NB):
            if j <= k:
                white[at(k, j)] = work[at(k, j)].astype(jnp.bfloat16)
            else:
                white[at(k, j)] = jnp.zeros((BLK, BLK), jnp.bfloat16)
    whitened = lax.dot_general(rows_ref[...], white[...], (((1,), (1,)), ((), ())),
                               preferred_element_type=jnp.float32).astype(jnp.bfloat16)
    widened = whitened.astype(jnp.float32)
    square_sum = jnp.sum(widened * widened, axis=1, keepdims=True)
    unit = (widened * lax.rsqrt(square_sum + 1e-06)).astype(jnp.bfloat16)
    sim = lax.dot_general(unit, unit, (((1,), (1,)), ((), ())), preferred_element_type=jnp.float32)
    slots = sim.shape[0]
    same = (idc_ref[...] == idr_ref[...]) & (idr_ref[...] >= 0)
    other = (lax.broadcasted_iota(jnp.int32, (slots, slots), 0)
             != lax.broadcasted_iota(jnp.int32, (slots, slots), 1))
    out_ref[...] = jnp.max(jnp.where(same & other, sim, -1.0), axis=0, keepdims=True)


def slot_scores(moments, rows, ids, row_total):
    slots = rows.shape[0]
    vm = pl.BlockSpec(memory_space=pltpu.VMEM)
    return pl.pallas_call(
        functools.partial(score_kernel, float(row_total)),
        out_shape=jax.ShapeDtypeStruct((1, slots), jnp.float32),
        in_specs=[vm] * 4,
        out_specs=vm,
        scratch_shapes=[pltpu.VMEM((D, D), jnp.float32), pltpu.VMEM((BLK, BLK), jnp.float32),
                        pltpu.VMEM((D, D), jnp.bfloat16)],
        name="scores",
    )(moments.reshape(NX, NC * NY * NZ, NB, BLK), rows, ids.reshape(1, slots),
      ids.reshape(slots, 1))


def local(embeddings, cluster_ids):
    row_count, feat_width = embeddings.shape
    dp_count = lax.axis_size("dp")
    mp_count = lax.axis_size("mp")
    mp_index = lax.axis_index("mp")
    pair_cap = 2 * row_count // dp_count
    slot_count = dp_count * pair_cap
    moments = summed_moments(embeddings)
    owner_ids = cluster_ids // CPO
    owner_hits = (owner_ids[:, None] == jnp.arange(dp_count, dtype=jnp.int32)[None, :]).astype(
        jnp.int32
    )
    earlier_hits = jnp.cumsum(owner_hits, axis=0) - owner_hits
    row_rank = jnp.sum(earlier_hits * owner_hits, axis=1)
    col_share = feat_width // mp_count
    part = lax.dynamic_slice_in_dim(embeddings, mp_index * col_share, col_share, 1)
    slot_index = owner_ids * pair_cap + row_rank
    send_rows = jnp.zeros((slot_count, col_share), jnp.bfloat16).at[slot_index].set(part)
    send_ids = jnp.full((slot_count,), -1, jnp.int32).at[slot_index].set(cluster_ids)
    got_rows, got_ids = (
        lax.all_to_all(send_rows, "dp", split_axis=0, concat_axis=0, tiled=True),
        lax.all_to_all(send_ids, "dp", split_axis=0, concat_axis=0, tiled=True),
    )
    key_rows = lax.all_gather(got_rows, "mp", axis=1, tiled=True)
    best = slot_scores(moments, key_rows, got_ids, row_count * dp_count)
    returned = lax.all_to_all(best.reshape(slot_count), "dp", split_axis=0, concat_axis=0, tiled=True)
    return returned[slot_index]


def solution(mesh):
    in_specs = (P("dp", None), P("dp"))
    out_specs = P("dp")
    return jax.shard_map(local, mesh=mesh, in_specs=in_specs, out_specs=out_specs, check_vma=False)
```

```python
import functools

import jax
import jax.numpy as jnp
from jax import lax
from jax.experimental import pallas as pl
from jax.experimental.pallas import tpu as pltpu
from jax.sharding import PartitionSpec as P

CPO = 4
NX, NC, NY, NZ = 4, 2, 4, 16
BLK = 128
NB = 6
D = NB * BLK
N_DP = NC * NY * NZ
PAIR = 4
GATHER_AT = 2
MESH = pl.DeviceIdType.MESH
HIGH = lax.Precision.HIGHEST


def lower_inverse(block):
    lane = lax.broadcasted_iota(jnp.int32, (8, BLK), 1)
    sub = lax.broadcasted_iota(jnp.int32, (8, BLK), 0)
    groups = BLK // 8
    wide = (8, BLK)
    scales = []
    for t in range(groups):
        own = block[t]
        base = 8 * t
        cols = [jnp.broadcast_to(own[:, base + q:base + q + 1], wide) for q in range(8)]
        piv = [[None] * 8 for _ in range(8)]
        for q in range(8):
            for r in range(q, 8):
                piv[q][r] = jnp.broadcast_to(cols[r][q:q + 1, :], wide)
        mult = [[None] * 8 for _ in range(8)]
        inv = [None] * 8
        scale = None
        for q in range(8):
            inv[q] = 1.0 / piv[q][q]
            for r in range(q + 1, 8):
                mult[q][r] = piv[q][r] * inv[q]
            for r in range(q + 1, 8):
                for s in range(r, 8):
                    piv[r][s] = piv[r][s] - mult[q][r] * piv[q][s]
            root = lax.rsqrt(piv[q][q])
            root = root * (1.5 - 0.5 * piv[q][q] * root * root)
            scale = root if scale is None else jnp.where(sub == q, root, scale)
        scales.append(scale)
        rows = []
        for q in range(8):
            row = jnp.broadcast_to(own[q:q + 1, :], wide)
            row = jnp.where(lane == base + q, inv[q], row * inv[q])
            rows.append(row)
            masked = jnp.where(sub > q, cols[q], 0.0)
            own = jnp.where((lane == base + q) & (sub > q), 0.0, own) - masked * row
            for r in range(q + 1, 8):
                cols[r] = cols[r] - masked * mult[q][r]
        block[t] = own
        for s in range(t + 1, groups):
            cur = block[s]
            coef = [jnp.broadcast_to(cur[:, base + q:base + q + 1], wide) for q in range(8)]
            for q in range(8):
                cur = jnp.where(lane == base + q, 0.0, cur) - coef[q] * rows[q]
                for r in range(q + 1, 8):
                    coef[r] = coef[r] - coef[q] * mult[q][r]
            block[s] = cur
    for t in range(groups):
        diff = lane - sub - 8 * t
        block[t] = scales[t] * jnp.where(diff < 0, block[t], jnp.where(diff == 0, 1.0, 0.0))
    return block


def tdot(a, b):
    return lax.dot_general(a, b, (((0,), (0,)), ((), ())), precision=HIGH,
                           preferred_element_type=jnp.float32)


def kernel(row_total, x_ref, ids_ref, out_ref,
           part, got_c, half, got_y, quarter, got_z, mom,
           stage, send_rows, got, work, diag, white, rows, ret, ret_got,
           c_send, c_recv, y_send, y_recv, z_send, z_recv,
           gz_send, gz_recv, a_send, a_recv, b_send, b_recv,
           a2_send, a2_recv, b2_send, b2_recv, gc_send, gc_recv,
           d_send, d_recv, x_send, x_recv, r_send, r_recv):
    f32, bf16 = jnp.float32, jnp.bfloat16
    m = lax.axis_index("mp")
    d = lax.axis_index("dp")
    c = lax.rem(d, 2)
    z = lax.rem(lax.div(d, 2), NZ)
    y = lax.div(d, 2 * NZ)

    def dev(yy, zz, cc, mm):
        return ((yy * NZ + zz) * 2 + cc, mm)

    sibling = dev(y, z, 1 - c, m)
    y_peers = [lax.rem(y + o, NY) for o in (2, 1, 3)]
    z_peers = [lax.rem(z + o, NZ) for o in (8, 7, 9, 6, 10, 5, 11, 4, 12, 3, 13, 2, 14, 1, 15)]
    x_peers = [lax.rem(m + o, NX) for o in (2, 1, 3)]
    barrier = pltpu.get_barrier_semaphore()

    @pl.loop(1, N_DP)
    def _(o):
        pl.semaphore_signal(barrier, inc=1, device_id=(lax.rem(d + o, N_DP), m),
                            device_id_type=MESH)
    for p in x_peers:
        pl.semaphore_signal(barrier, inc=1, device_id=(d, p), device_id_type=MESH)

    for i in range(NB):
        j = lax.rem(i + m, NB)
        left = x_ref[:, i * BLK:(i + 1) * BLK]
        right = x_ref[:, pl.ds(pl.multiple_of(j * BLK, BLK), BLK)]
        prod = lax.dot_general(left, right, (((0,), (0,)), ((), ())),
                               preferred_element_type=f32)
        part[:, :, :, i, :] = prod.reshape(NC, NY, NZ, BLK)

    count = x_ref.shape[0]
    owner = lax.div(ids_ref[...], CPO)
    within = (ids_ref[...] - owner * CPO + 1).astype(f32)
    owner = owner.astype(f32)
    owner_row = jnp.broadcast_to(owner, (count, count))
    first = lax.broadcasted_iota(jnp.int32, (count, count), 0)
    second = lax.broadcasted_iota(jnp.int32, (count, count), 1)
    earlier = (owner_row == owner_row.T) & (first < second)
    rank = jnp.sum(jnp.where(earlier, 1.0, 0.0), axis=0, keepdims=True)
    owner_iota = lax.broadcasted_iota(jnp.int32, (N_DP, count), 0).astype(f32)
    own_hit = owner_iota == owner
    pick = jnp.where(own_hit & (rank == m.astype(f32)), 1.0, 0.0)
    picked = lax.dot_general(pick.astype(bf16), x_ref[...], (((1,), (0,)), ((), ())),
                             preferred_element_type=f32)
    label = jnp.sum(pick * within, axis=1, keepdims=True) - 1.0
    for i in range(NB):
        stage[:, i, :] = picked[:, i * BLK:(i + 1) * BLK]
    stage[:, NB, :] = jnp.broadcast_to(label, (N_DP, BLK))
    stage[:, NB + 1, :] = jnp.zeros((N_DP, BLK), f32)
    send_rows[...] = stage[...].astype(bf16)
    got[m, d] = send_rows[d]
    pl.semaphore_wait(barrier, N_DP - 1 + NX - 1)

    def copy(src, dst, send, recv, device):
        return pltpu.make_async_remote_copy(
            src_ref=src, dst_ref=dst, send_sem=send, recv_sem=recv,
            device_id=device, device_id_type=MESH)

    cc = copy(part.at[1 - c], got_c, c_send, c_recv, sibling)
    cc.start()
    cc.wait_recv()
    half[...] = part[c] + got_c[...]
    sent = []
    for p in y_peers:
        cp = copy(half.at[p], got_y.at[y], y_send.at[p], y_recv.at[y], dev(p, z, c, m))
        cp.start()
        sent.append(cp)
    total = half[y]
    for p in y_peers:
        copy(half.at[p], got_y.at[p], y_send.at[p], y_recv.at[p], dev(p, z, c, m)).wait_recv()
        total = total + got_y[p]
    quarter[...] = total
    for p in z_peers:
        cp = copy(quarter.at[p], got_z.at[z], z_send.at[p], z_recv.at[z], dev(y, p, c, m))
        cp.start()
        sent.append(cp)
    row = quarter[z]
    for p in reversed(z_peers):
        copy(quarter.at[p], got_z.at[p], z_send.at[p], z_recv.at[p], dev(y, p, c, m)).wait_recv()
        row = row + got_z[p]
    mom[m, c, y, z] = row
    for p in z_peers:
        cp = copy(mom.at[m, c, y, z], mom.at[m, c, y, z], gz_send.at[p], gz_recv.at[z],
                  dev(y, p, c, m))
        cp.start()
        sent.append(cp)

    @pl.loop(1, N_DP)
    def _(o):
        p = lax.rem(d + o, N_DP)
        copy(send_rows.at[p], got.at[m, d], d_send, d_recv, (p, m)).start()
    for p in reversed(z_peers):
        copy(mom.at[m, c, y, p], mom.at[m, c, y, p], gz_send.at[p], gz_recv.at[p],
             dev(y, p, c, m)).wait_recv()
    lo, hi = pl.ds(0, NZ // 2), pl.ds(NZ // 2, NZ // 2)
    for p in y_peers:
        cp = copy(mom.at[m, c, y, lo], mom.at[m, c, y, lo], a_send.at[p], a_recv.at[y],
                  dev(p, z, c, m))
        cp.start()
        sent.append(cp)
    for p in x_peers:
        cp = copy(mom.at[m, c, y, hi], mom.at[m, c, y, hi], b_send.at[p], b_recv.at[m],
                  dev(y, z, c, p))
        cp.start()
        sent.append(cp)
    for p in y_peers:
        copy(mom.at[m, c, p, lo], mom.at[m, c, p, lo], a_send.at[p], a_recv.at[p],
             dev(p, z, c, m)).wait_recv()
    for p in x_peers:
        cp = copy(mom.at[m, c, :, lo], mom.at[m, c, :, lo], a2_send.at[p], a2_recv.at[m],
                  dev(y, z, c, p))
        cp.start()
        sent.append(cp)
    for p in x_peers:
        copy(mom.at[p, c, y, hi], mom.at[p, c, y, hi], b_send.at[p], b_recv.at[p],
             dev(y, z, c, p)).wait_recv()
    for p in y_peers:
        cp = copy(mom.at[:, c, y, hi], mom.at[:, c, y, hi], b2_send.at[p], b2_recv.at[y],
                  dev(p, z, c, m))
        cp.start()
        sent.append(cp)
    for p in x_peers:
        copy(mom.at[p, c, :, lo], mom.at[p, c, :, lo], a2_send.at[p], a2_recv.at[p],
             dev(y, z, c, p)).wait_recv()
    for p in y_peers:
        copy(mom.at[:, c, p, hi], mom.at[:, c, p, hi], b2_send.at[p], b2_recv.at[p],
             dev(p, z, c, m)).wait_recv()
    gc = copy(mom.at[:, c], mom.at[:, c], gc_send, gc_recv, sibling)
    gc.start()
    copy(mom.at[:, 1 - c], mom.at[:, 1 - c], gc_send, gc_recv, sibling).wait_recv()
    cc.wait_send()
    for cp in sent:
        cp.wait_send()
    gc.wait_send()

    scale = 1.0 / row_total
    eye = jnp.where(lax.broadcasted_iota(jnp.int32, (BLK, BLK), 0)
                    == lax.broadcasted_iota(jnp.int32, (BLK, BLK), 1), 0.001, 0.0)

    def at(i, j):
        return (slice(i * BLK, (i + 1) * BLK), slice(j * BLK, (j + 1) * BLK))

    def moment_block(g, i):
        return mom[g, :, :, :, i, :].reshape(BLK, BLK) * scale

    for i in range(NB):
        for g in range(4):
            j = i + g
            if j < NB:
                val = moment_block(g, i)
                work[at(i, j)] = val + eye if g == 0 else val
            elif g < 3:
                work[at(j - NB, i)] = moment_block(g, i).T

    @pl.loop(0, NB)
    def _(k):
        for kk in range(NB):
            @pl.when(k == kk)
            def _():
                diag[...] = work[at(kk, kk)]
                if kk == GATHER_AT:
                    copy(send_rows.at[pl.ds(0, N_DP - 1)], got.at[m, pl.ds(0, N_DP - 1)],
                         d_send, d_recv, sibling).wait()
                    for p in x_peers:
                        copy(got.at[m], got.at[m], x_send.at[p], x_recv.at[m],
                             (d, p)).start()
        block = lower_inverse([diag[8 * t:8 * t + 8, :] for t in range(BLK // 8)])
        for t in range(BLK // 8):
            diag[8 * t:8 * t + 8, :] = block[t]
        for kk in range(NB):
            @pl.when(k == kk)
            def _():
                rk = slice(kk * BLK, (kk + 1) * BLK)
                inverse = diag[...]
                line = lax.dot_general(inverse, work[rk, :], (((1,), (0,)), ((), ())),
                                       precision=HIGH, preferred_element_type=f32)
                work[rk, :] = line
                work[at(kk, kk)] = inverse
                for i in range(kk + 1, NB):
                    ri = slice(i * BLK, (i + 1) * BLK)
                    left = work[at(kk, i)]
                    if kk:
                        work[ri, :kk * BLK] = work[ri, :kk * BLK] - tdot(left, work[rk, :kk * BLK])
                    work[at(i, kk)] = -tdot(left, inverse)
                    work[ri, i * BLK:] = work[ri, i * BLK:] - tdot(left, work[rk, i * BLK:])

    for k in range(NB):
        for j in range(NB):
            if j <= k:
                white[at(k, j)] = work[at(k, j)].astype(bf16)
            else:
                white[at(k, j)] = jnp.zeros((BLK, BLK), bf16)

    for p in x_peers:
        copy(got.at[p], got.at[p], x_send.at[p], x_recv.at[p], (d, p)).wait()
    labels = []
    for k in range(PAIR):
        stage[...] = got[k].astype(f32)
        for i in range(NB):
            rows[k * N_DP:(k + 1) * N_DP, i * BLK:(i + 1) * BLK] = stage[:, i, :].astype(bf16)
        labels.append(stage[:, NB, :])
    whitened = lax.dot_general(rows[...], white[...], (((1,), (1,)), ((), ())),
                               preferred_element_type=f32).astype(bf16)
    widened = whitened.astype(f32)
    square_sum = jnp.sum(widened * widened, axis=1, keepdims=True)
    rows[...] = (widened * lax.rsqrt(square_sum + 1e-06)).astype(bf16)
    lane = lax.broadcasted_iota(jnp.int32, (N_DP, N_DP), 1)
    other = lax.broadcasted_iota(jnp.int32, (N_DP, N_DP), 0) != lane
    flipped = [value.T for value in labels]
    reply = jnp.zeros((N_DP, N_DP), f32)
    for a in range(PAIR):
        sim = lax.dot_general(rows[a * N_DP:(a + 1) * N_DP, :], rows[...],
                              (((1,), (1,)), ((), ())), preferred_element_type=f32)
        best = jnp.full((N_DP, N_DP), -1.0, f32)
        for b in range(PAIR):
            same = (labels[a] == flipped[b]) & (labels[a] >= 0.0)
            if a == b:
                same = same & other
            best = jnp.maximum(best, jnp.where(same, sim[:, b * N_DP:(b + 1) * N_DP], -1.0))
        reply = jnp.where(lane == a, jnp.max(best, axis=1, keepdims=True), reply)
    ret[:, 0, :] = reply
    ret_got[d] = ret[d]

    @pl.loop(1, N_DP)
    def _(o):
        p = lax.rem(d + o, N_DP)
        copy(ret.at[p], ret_got.at[d], r_send, r_recv, (p, m)).start()
    copy(ret.at[pl.ds(0, N_DP - 1)], ret_got.at[pl.ds(0, N_DP - 1)], r_send, r_recv,
         sibling).wait()
    table = lax.dot_general(ret_got[:, 0, :], jnp.where(own_hit, 1.0, 0.0),
                            (((0,), (0,)), ((), ())), precision=HIGH, preferred_element_type=f32)
    score = jnp.zeros((1, count), f32)
    for k in range(PAIR):
        score = jnp.where(rank == float(k), table[k:k + 1, :], score)
    out_ref[...] = score


def local(embeddings, cluster_ids):
    row_count, feat_width = embeddings.shape
    dp_count = lax.axis_size("dp")
    f32, bf16 = jnp.float32, jnp.bfloat16
    dma = pltpu.SemaphoreType.DMA
    scratch = [
        pltpu.VMEM((NC, NY, NZ, NB, BLK), f32),
        pltpu.VMEM((NY, NZ, NB, BLK), f32),
        pltpu.VMEM((NY, NZ, NB, BLK), f32),
        pltpu.VMEM((NY, NZ, NB, BLK), f32),
        pltpu.VMEM((NZ, NB, BLK), f32),
        pltpu.VMEM((NZ, NB, BLK), f32),
        pltpu.VMEM((NX, NC, NY, NZ, NB, BLK), f32),
        pltpu.VMEM((N_DP, NB + 2, BLK), f32),
        pltpu.VMEM((N_DP, NB + 2, BLK), bf16),
        pltpu.VMEM((NX, N_DP, NB + 2, BLK), bf16),
        pltpu.VMEM((D, D), f32),
        pltpu.VMEM((BLK, BLK), f32),
        pltpu.VMEM((D, D), bf16),
        pltpu.VMEM((PAIR * N_DP, D), bf16),
        pltpu.VMEM((N_DP, 1, BLK), f32),
        pltpu.VMEM((N_DP, 1, BLK), f32),
        dma, dma, dma((NY,)), dma((NY,)), dma((NZ,)), dma((NZ,)),
        dma((NZ,)), dma((NZ,)), dma((NY,)), dma((NY,)), dma((NX,)), dma((NX,)),
        dma((NX,)), dma((NX,)), dma((NY,)), dma((NY,)), dma, dma,
        dma, dma, dma((NX,)), dma((NX,)), dma, dma,
    ]
    vm = pl.BlockSpec(memory_space=pltpu.VMEM)
    scores = pl.pallas_call(
        functools.partial(kernel, float(row_count * dp_count)),
        out_shape=jax.ShapeDtypeStruct((1, row_count), f32),
        in_specs=[vm, vm],
        out_specs=vm,
        scratch_shapes=scratch,
        name="dedup",
        compiler_params=pltpu.CompilerParams(collective_id=0, has_side_effects=True),
    )(embeddings, cluster_ids.reshape(1, row_count))
    return scores.reshape(row_count)


def solution(mesh):
    in_specs = (P("dp", None), P("dp"))
    out_specs = P("dp")
    return jax.shard_map(local, mesh=mesh, in_specs=in_specs, out_specs=out_specs, check_vma=False)
```

```python
import functools

import jax
import jax.numpy as jnp
from jax import lax
from jax.experimental import pallas as pl
from jax.experimental.pallas import tpu as pltpu
from jax.sharding import PartitionSpec as P

CPO = 4
NX, NC, NY, NZ = 4, 2, 4, 16
BLK = 128
NB = 6
D = NB * BLK
N_DP = NC * NY * NZ
PAIR = 4
GATHER_AT = 1
MESH = pl.DeviceIdType.MESH
HIGH = lax.Precision.HIGHEST


def split3(value):
    high = value.astype(jnp.bfloat16)
    rest = value - high.astype(jnp.float32)
    mid = rest.astype(jnp.bfloat16)
    low = (rest - mid.astype(jnp.float32)).astype(jnp.bfloat16)
    return high, mid, low


def lower_inverse(block):
    lane = lax.broadcasted_iota(jnp.int32, (8, BLK), 1)
    sub = lax.broadcasted_iota(jnp.int32, (8, BLK), 0)
    groups = BLK // 8
    wide = (8, BLK)
    scales = []
    for t in range(groups):
        own = block[t]
        base = 8 * t
        cols = [jnp.broadcast_to(own[:, base + q:base + q + 1], wide) for q in range(8)]
        piv = [[None] * 8 for _ in range(8)]
        for q in range(8):
            for r in range(q, 8):
                piv[q][r] = jnp.broadcast_to(cols[r][q:q + 1, :], wide)
        mult = [[None] * 8 for _ in range(8)]
        inv = [None] * 8
        scale = None
        for q in range(8):
            inv[q] = 1.0 / piv[q][q]
            for r in range(q + 1, 8):
                mult[q][r] = piv[q][r] * inv[q]
            for r in range(q + 1, 8):
                for s in range(r, 8):
                    piv[r][s] = piv[r][s] - mult[q][r] * piv[q][s]
            root = lax.rsqrt(piv[q][q])
            root = root * (1.5 - 0.5 * piv[q][q] * root * root)
            scale = root if scale is None else jnp.where(sub == q, root, scale)
        scales.append(scale)
        rows = []
        for q in range(8):
            row = jnp.broadcast_to(own[q:q + 1, :], wide)
            row = jnp.where(lane == base + q, inv[q], row * inv[q])
            rows.append(row)
            masked = jnp.where(sub > q, cols[q], 0.0)
            own = jnp.where((lane == base + q) & (sub > q), 0.0, own) - masked * row
            for r in range(q + 1, 8):
                cols[r] = cols[r] - masked * mult[q][r]
        block[t] = own
        if t + 1 == groups:
            continue
        cur = block[t + 1]
        coef = [jnp.broadcast_to(cur[:, base + q:base + q + 1], wide) for q in range(8)]
        for q in range(8):
            cur = jnp.where(lane == base + q, 0.0, cur) - coef[q] * rows[q]
            for r in range(q + 1, 8):
                coef[r] = coef[r] - coef[q] * mult[q][r]
        block[t + 1] = cur
        if t + 2 == groups:
            continue
        panel = (lane >= base) & (lane < base + 8)
        rows = [jnp.where((lane > base + q) & (lane < base + 8), 0.0, rows[q]) for q in range(8)]
        right = rows[0]
        for q in range(1, 8):
            right = jnp.where(sub == q, rows[q], right)
        ah, am, al = split3(own)
        bh, bm, bl = split3(right)
        upd = lax.dot_general(jnp.concatenate([ah, ah, am, ah, al, am], axis=0),
                              jnp.concatenate([bh, bm, bh, bl, bh, bm], axis=0),
                              (((0,), (0,)), ((), ())), preferred_element_type=jnp.float32)
        for s in range(t + 2, groups):
            block[s] = jnp.where(panel, 0.0, block[s]) - upd[8 * s:8 * s + 8, :]
    for t in range(groups):
        diff = lane - sub - 8 * t
        block[t] = scales[t] * jnp.where(diff < 0, block[t], jnp.where(diff == 0, 1.0, 0.0))
    return block


def stack_left(value, axis):
    high, mid, low = split3(value)
    return jnp.concatenate([high, high, mid, high, low, mid], axis=axis)


def stack_right(value, axis):
    high, mid, low = split3(value)
    return jnp.concatenate([high, mid, high, low, high, mid], axis=axis)


def mm(a, b):
    return lax.dot_general(a, b, (((1,), (0,)), ((), ())), preferred_element_type=jnp.float32)


def kernel(row_total, x_ref, ids_ref, out_ref,
           part, got_c, half, got_y, quarter, got_z, mom,
           stage, send_rows, between, got, work, diag, left, right, white, rows,
           ret, ret_between, ret_got,
           c_send, c_recv, y_send, y_recv, z_send, z_recv,
           gz_send, gz_recv, a_send, a_recv, b_send, b_recv,
           a2_send, a2_recv, b2_send, b2_recv, gc_send, gc_recv,
           d_send, d_recv, e_send, e_recv, x_send, x_recv,
           r_send, r_recv, t_send, t_recv):
    f32, bf16 = jnp.float32, jnp.bfloat16
    m = lax.axis_index("mp")
    d = lax.axis_index("dp")
    c = lax.rem(d, 2)
    z = lax.rem(lax.div(d, 2), NZ)
    y = lax.div(d, 2 * NZ)

    def dev(yy, zz, cc, mm):
        return ((yy * NZ + zz) * 2 + cc, mm)

    sibling = dev(y, z, 1 - c, m)
    y_peers = [lax.rem(y + o, NY) for o in (2, 1, 3)]
    z_peers = [lax.rem(z + o, NZ) for o in (8, 7, 9, 6, 10, 5, 11, 4, 12, 3, 13, 2, 14, 1, 15)]
    x_peers = [lax.rem(m + o, NX) for o in (2, 1, 3)]
    plane = [(lax.rem(y + o, NY), co) for o in (2, 1, 3) for co in (1 - c, c)] + [(y, 1 - c)]
    barrier = pltpu.get_barrier_semaphore()
    everyone = ([dev(y, p, c, m) for p in z_peers] + [dev(yy, z, co, m) for yy, co in plane]
                + [dev(y, z, c, p) for p in x_peers])
    for peer in everyone:
        pl.semaphore_signal(barrier, inc=1, device_id=peer, device_id_type=MESH)

    for i in range(NB):
        j = lax.rem(i + m, NB)
        lhs = x_ref[:, i * BLK:(i + 1) * BLK]
        rhs = x_ref[:, pl.ds(pl.multiple_of(j * BLK, BLK), BLK)]
        prod = lax.dot_general(lhs, rhs, (((0,), (0,)), ((), ())),
                               preferred_element_type=f32)
        part[:, :, :, i, :] = prod.reshape(NC, NY, NZ, BLK)

    count = x_ref.shape[0]
    owner = lax.div(ids_ref[...], CPO)
    within = (ids_ref[...] - owner * CPO + 1).astype(f32)
    owner = owner.astype(f32)
    owner_row = jnp.broadcast_to(owner, (count, count))
    first = lax.broadcasted_iota(jnp.int32, (count, count), 0)
    second = lax.broadcasted_iota(jnp.int32, (count, count), 1)
    earlier = (owner_row == owner_row.T) & (first < second)
    rank = jnp.sum(jnp.where(earlier, 1.0, 0.0), axis=0, keepdims=True)
    owner_iota = lax.broadcasted_iota(jnp.int32, (N_DP, count), 0).astype(f32)
    pick = jnp.where((owner_iota == owner) & (rank == m.astype(f32)), 1.0, 0.0)
    picked = lax.dot_general(pick.astype(bf16), x_ref[...], (((1,), (0,)), ((), ())),
                             preferred_element_type=f32)
    label = jnp.sum(pick * within, axis=1, keepdims=True) - 1.0
    for i in range(NB):
        stage[:, i, :] = picked[:, i * BLK:(i + 1) * BLK]
    stage[:, NB, :] = jnp.broadcast_to(label, (N_DP, BLK))
    stage[:, NB + 1, :] = jnp.zeros((N_DP, BLK), f32)
    send_rows[...] = stage[...].astype(bf16).reshape(NY, NZ, NC, NB + 2, BLK)
    between[y, c] = send_rows[y, :, c]
    pl.semaphore_wait(barrier, len(everyone))

    def copy(src, dst, send, recv, device):
        return pltpu.make_async_remote_copy(
            src_ref=src, dst_ref=dst, send_sem=send, recv_sem=recv,
            device_id=device, device_id_type=MESH)

    cc = copy(part.at[1 - c], got_c, c_send, c_recv, sibling)
    cc.start()
    cc.wait_recv()
    half[...] = part[c] + got_c[...]
    sent = []
    for p in y_peers:
        cp = copy(half.at[p], got_y.at[y], y_send.at[p], y_recv.at[y], dev(p, z, c, m))
        cp.start()
        sent.append(cp)
    total = half[y]
    for p in y_peers:
        copy(half.at[p], got_y.at[p], y_send.at[p], y_recv.at[p], dev(p, z, c, m)).wait_recv()
        total = total + got_y[p]
    quarter[...] = total
    for p in z_peers:
        cp = copy(quarter.at[p], got_z.at[z], z_send.at[p], z_recv.at[z], dev(y, p, c, m))
        cp.start()
        sent.append(cp)
    for yy, co in plane:
        cp = copy(send_rows.at[yy, :, co], between.at[y, c], d_send.at[yy * NC + co],
                  d_recv.at[y * NC + c], dev(yy, z, co, m))
        cp.start()
        sent.append(cp)
    row = quarter[z]
    for p in reversed(z_peers):
        copy(quarter.at[p], got_z.at[p], z_send.at[p], z_recv.at[p], dev(y, p, c, m)).wait_recv()
        row = row + got_z[p]
    mom[m, c, y, z] = row
    for p in z_peers:
        cp = copy(mom.at[m, c, y, z], mom.at[m, c, y, z], gz_send.at[p], gz_recv.at[z],
                  dev(y, p, c, m))
        cp.start()
        sent.append(cp)

    for p in reversed(z_peers):
        copy(mom.at[m, c, y, p], mom.at[m, c, y, p], gz_send.at[p], gz_recv.at[p],
             dev(y, p, c, m)).wait_recv()
    for yy, co in plane:
        copy(send_rows.at[yy, :, co], between.at[yy, co], d_send.at[yy * NC + co],
             d_recv.at[yy * NC + co], dev(yy, z, co, m)).wait_recv()
    late = []
    for p in z_peers:
        cp = copy(between.at[:, :, p], got.at[m, :, :, z], e_send.at[p], e_recv.at[z],
                  dev(y, p, c, m))
        cp.start()
        late.append(cp)
    got[m, :, :, z] = between[:, :, z]
    lo, hi = pl.ds(0, NZ // 2), pl.ds(NZ // 2, NZ // 2)
    for p in y_peers:
        cp = copy(mom.at[m, c, y, lo], mom.at[m, c, y, lo], a_send.at[p], a_recv.at[y],
                  dev(p, z, c, m))
        cp.start()
        sent.append(cp)
    for p in x_peers:
        cp = copy(mom.at[m, c, y, hi], mom.at[m, c, y, hi], b_send.at[p], b_recv.at[m],
                  dev(y, z, c, p))
        cp.start()
        sent.append(cp)
    for p in y_peers:
        copy(mom.at[m, c, p, lo], mom.at[m, c, p, lo], a_send.at[p], a_recv.at[p],
             dev(p, z, c, m)).wait_recv()
    for p in x_peers:
        cp = copy(mom.at[m, c, :, lo], mom.at[m, c, :, lo], a2_send.at[p], a2_recv.at[m],
                  dev(y, z, c, p))
        cp.start()
        sent.append(cp)
    for p in x_peers:
        copy(mom.at[p, c, y, hi], mom.at[p, c, y, hi], b_send.at[p], b_recv.at[p],
             dev(y, z, c, p)).wait_recv()
    for p in y_peers:
        cp = copy(mom.at[:, c, y, hi], mom.at[:, c, y, hi], b2_send.at[p], b2_recv.at[y],
                  dev(p, z, c, m))
        cp.start()
        sent.append(cp)
    for p in x_peers:
        copy(mom.at[p, c, :, lo], mom.at[p, c, :, lo], a2_send.at[p], a2_recv.at[p],
             dev(y, z, c, p)).wait_recv()
    for p in y_peers:
        copy(mom.at[:, c, p, hi], mom.at[:, c, p, hi], b2_send.at[p], b2_recv.at[p],
             dev(p, z, c, m)).wait_recv()
    gc = copy(mom.at[:, c], mom.at[:, c], gc_send, gc_recv, sibling)
    gc.start()
    copy(mom.at[:, 1 - c], mom.at[:, 1 - c], gc_send, gc_recv, sibling).wait_recv()
    cc.wait_send()
    for cp in sent:
        cp.wait_send()
    gc.wait_send()

    for i in range(0, NB, 2):
        white[i * BLK:(i + 1) * BLK, (i + 1) * BLK:(i + 2) * BLK] = jnp.zeros((BLK, BLK), bf16)
    scale = 1.0 / row_total
    eye = jnp.where(lax.broadcasted_iota(jnp.int32, (BLK, BLK), 0)
                    == lax.broadcasted_iota(jnp.int32, (BLK, BLK), 1), 0.001, 0.0)

    def at(i, j):
        return (slice(i * BLK, (i + 1) * BLK), slice(j * BLK, (j + 1) * BLK))

    def moment_block(g, i):
        return mom[g, :, :, :, i, :].reshape(BLK, BLK) * scale

    for i in range(NB):
        for g in range(4):
            j = i + g
            if j < NB:
                val = moment_block(g, i)
                work[at(i, j)] = val + eye if g == 0 else val
            elif g < 3:
                work[at(j - NB, i)] = moment_block(g, i).T

    @pl.loop(0, NB)
    def _(k):
        for kk in range(NB):
            @pl.when(k == kk)
            def _():
                diag[...] = work[at(kk, kk)]
                if kk == GATHER_AT:
                    for p in z_peers:
                        copy(between.at[:, :, p], got.at[m, :, :, p], e_send.at[p], e_recv.at[p],
                             dev(y, p, c, m)).wait_recv()
                    for p in x_peers:
                        copy(got.at[m], got.at[m], x_send.at[p], x_recv.at[m],
                             (d, p)).start()
        block = lower_inverse([diag[8 * t:8 * t + 8, :] for t in range(BLK // 8)])
        for t in range(BLK // 8):
            diag[8 * t:8 * t + 8, :] = block[t]
        for kk in range(NB):
            @pl.when(k == kk)
            def _():
                rk = slice(kk * BLK, (kk + 1) * BLK)
                inverse = diag[...]
                line = mm(stack_left(inverse, 1), stack_right(work[rk, :], 0))
                white[at(kk, kk)] = inverse.astype(bf16)
                if kk:
                    white[rk, :kk * BLK] = line[:, :kk * BLK].astype(bf16)
                if kk == NB - 1:
                    return
                done = (kk + 1) * BLK
                left[done:, :] = stack_left(line[:, done:].T, 1)
                right[:, :kk * BLK + BLK] = stack_right(
                    jnp.concatenate([line[:, :kk * BLK], inverse], axis=1) if kk else inverse, 0)
                right[:, done:] = stack_right(line[:, done:], 0)
                old = mm(left[done:, :], right[:, :done])
                if kk:
                    work[done:, :kk * BLK] = work[done:, :kk * BLK] - old[:, :kk * BLK]
                work[done:, rk] = -old[:, rk]
                for i in range(kk + 1, NB, 2):
                    ri = slice(i * BLK, min(i + 2, NB) * BLK)
                    work[ri, i * BLK:] = work[ri, i * BLK:] - mm(left[ri, :], right[:, i * BLK:])

    for p in x_peers:
        copy(got.at[p], got.at[p], x_send.at[p], x_recv.at[p], (d, p)).wait()
    for cp in late:
        cp.wait_send()
    labels = []
    for k in range(PAIR):
        stage[...] = got[k].reshape(N_DP, NB + 2, BLK).astype(f32)
        for i in range(NB):
            rows[k * N_DP:(k + 1) * N_DP, i * BLK:(i + 1) * BLK] = stage[:, i, :].astype(bf16)
        labels.append(stage[:, NB, :])
    wide = 2 * BLK
    whitened = jnp.concatenate(
        [lax.dot_general(rows[:, :n + wide], white[n:n + wide, :n + wide],
                         (((1,), (1,)), ((), ())), preferred_element_type=f32)
         for n in range(0, D, wide)], axis=1).astype(bf16)
    widened = whitened.astype(f32)
    square_sum = jnp.sum(widened * widened, axis=1, keepdims=True)
    rows[...] = (widened * lax.rsqrt(square_sum + 1e-06)).astype(bf16)
    lane = lax.broadcasted_iota(jnp.int32, (N_DP, N_DP), 1)
    other = lax.broadcasted_iota(jnp.int32, (N_DP, N_DP), 0) != lane
    flipped = [value.T for value in labels]
    reply = jnp.zeros((N_DP, N_DP), f32)
    for a in range(PAIR):
        sim = lax.dot_general(rows[a * N_DP:(a + 1) * N_DP, :], rows[...],
                              (((1,), (1,)), ((), ())), preferred_element_type=f32)
        best = jnp.full((N_DP, N_DP), -1.0, f32)
        for b in range(PAIR):
            same = (labels[a] == flipped[b]) & (labels[a] >= 0.0)
            if a == b:
                same = same & other
            best = jnp.maximum(best, jnp.where(same, sim[:, b * N_DP:(b + 1) * N_DP], -1.0))
        reply = jnp.where(lane == a, jnp.max(best, axis=1, keepdims=True), reply)
    ret[:, :, :, 0, :] = reply.reshape(NY, NC, NZ, BLK)
    back = []
    for p in z_peers:
        cp = copy(ret.at[:, :, p], ret_between.at[z], r_send.at[p], r_recv.at[z], dev(y, p, c, m))
        cp.start()
        back.append(cp)
    ret_between[z] = ret[:, :, z]
    for p in reversed(z_peers):
        copy(ret.at[:, :, p], ret_between.at[p], r_send.at[p], r_recv.at[p],
             dev(y, p, c, m)).wait_recv()
    for yy, co in plane:
        cp = copy(ret_between.at[:, yy, co], ret_got.at[y, c], t_send.at[yy * NC + co],
                  t_recv.at[y * NC + c], dev(yy, z, co, m))
        cp.start()
        back.append(cp)
    ret_got[y, c] = ret_between[:, y, c]
    spot = lax.broadcasted_iota(jnp.int32, (N_DP, count), 0)
    spot_z, spot_yc = lax.rem(spot, NZ), lax.div(spot, NZ)
    spot = (lax.div(spot_yc, NC) * NZ + spot_z) * NC + lax.rem(spot_yc, NC)
    hit = jnp.where(spot.astype(f32) == owner, 1.0, 0.0)
    for yy, co in plane:
        copy(ret_between.at[:, yy, co], ret_got.at[yy, co], t_send.at[yy * NC + co],
             t_recv.at[yy * NC + co], dev(yy, z, co, m)).wait_recv()
    for cp in back:
        cp.wait_send()
    table = lax.dot_general(ret_got[:, :, :, 0, :].reshape(N_DP, BLK), hit,
                            (((0,), (0,)), ((), ())), precision=HIGH, preferred_element_type=f32)
    score = jnp.zeros((1, count), f32)
    for k in range(PAIR):
        score = jnp.where(rank == float(k), table[k:k + 1, :], score)
    out_ref[...] = score


def local(embeddings, cluster_ids):
    row_count, feat_width = embeddings.shape
    dp_count = lax.axis_size("dp")
    f32, bf16 = jnp.float32, jnp.bfloat16
    dma = pltpu.SemaphoreType.DMA
    scratch = [
        pltpu.VMEM((NC, NY, NZ, NB, BLK), f32),
        pltpu.VMEM((NY, NZ, NB, BLK), f32),
        pltpu.VMEM((NY, NZ, NB, BLK), f32),
        pltpu.VMEM((NY, NZ, NB, BLK), f32),
        pltpu.VMEM((NZ, NB, BLK), f32),
        pltpu.VMEM((NZ, NB, BLK), f32),
        pltpu.VMEM((NX, NC, NY, NZ, NB, BLK), f32),
        pltpu.VMEM((N_DP, NB + 2, BLK), f32),
        pltpu.VMEM((NY, NZ, NC, NB + 2, BLK), bf16),
        pltpu.VMEM((NY, NC, NZ, NB + 2, BLK), bf16),
        pltpu.VMEM((NX, NY, NC, NZ, NB + 2, BLK), bf16),
        pltpu.VMEM((D, D), f32),
        pltpu.VMEM((BLK, BLK), f32),
        pltpu.VMEM((D, 6 * BLK), bf16),
        pltpu.VMEM((6 * BLK, D), bf16),
        pltpu.VMEM((D, D), bf16),
        pltpu.VMEM((PAIR * N_DP, D), bf16),
        pltpu.VMEM((NY, NC, NZ, 1, BLK), f32),
        pltpu.VMEM((NZ, NY, NC, 1, BLK), f32),
        pltpu.VMEM((NY, NC, NZ, 1, BLK), f32),
        dma, dma, dma((NY,)), dma((NY,)), dma((NZ,)), dma((NZ,)),
        dma((NZ,)), dma((NZ,)), dma((NY,)), dma((NY,)), dma((NX,)), dma((NX,)),
        dma((NX,)), dma((NX,)), dma((NY,)), dma((NY,)), dma, dma,
        dma((NY * NC,)), dma((NY * NC,)), dma((NZ,)), dma((NZ,)), dma((NX,)), dma((NX,)),
        dma((NZ,)), dma((NZ,)), dma((NY * NC,)), dma((NY * NC,)),
    ]
    vm = pl.BlockSpec(memory_space=pltpu.VMEM)
    scores = pl.pallas_call(
        functools.partial(kernel, float(row_count * dp_count)),
        out_shape=jax.ShapeDtypeStruct((1, row_count), f32),
        in_specs=[vm, vm],
        out_specs=vm,
        scratch_shapes=scratch,
        name="dedup",
        compiler_params=pltpu.CompilerParams(collective_id=0, has_side_effects=True),
    )(embeddings, cluster_ids.reshape(1, row_count))
    return scores.reshape(row_count)


def solution(mesh):
    in_specs = (P("dp", None), P("dp"))
    out_specs = P("dp")
    return jax.shard_map(local, mesh=mesh, in_specs=in_specs, out_specs=out_specs, check_vma=False)
```

```python
import functools

import jax
import jax.numpy as jnp
from jax import lax
from jax.experimental import pallas as pl
from jax.experimental.pallas import tpu as pltpu
from jax.sharding import PartitionSpec as P

CPO = 4
NX, NC, NY, NZ = 4, 2, 4, 16
BLK = 128
NB = 6
D = NB * BLK
N_DP = NC * NY * NZ
PAIR = 4
GATHER_AT = 1
MESH = pl.DeviceIdType.MESH
HIGH = lax.Precision.HIGHEST


def split3(value):
    high = value.astype(jnp.bfloat16)
    rest = value - high.astype(jnp.float32)
    mid = rest.astype(jnp.bfloat16)
    low = (rest - mid.astype(jnp.float32)).astype(jnp.bfloat16)
    return high, mid, low


def lower_inverse(block):
    lane = lax.broadcasted_iota(jnp.int32, (8, BLK), 1)
    sub = lax.broadcasted_iota(jnp.int32, (8, BLK), 0)
    groups = BLK // 8
    wide = (8, BLK)
    picks = [jnp.full(wide, q, jnp.int32) for q in range(8)]
    scales = []
    for t in range(groups):
        own = block[t]
        base = 8 * t
        cols = [jnp.broadcast_to(own[:, base + q:base + q + 1], wide) for q in range(8)]
        piv = [[None] * 8 for _ in range(8)]
        for q in range(8):
            for r in range(q, 8):
                piv[q][r] = jnp.take_along_axis(cols[r], picks[q], axis=0)
        mult = [[None] * 8 for _ in range(8)]
        inv = [None] * 8
        scale = None
        for q in range(0, 8, 2):
            cross, last = piv[q][q + 1], piv[q + 1][q + 1]
            minor = piv[q][q] * last - cross * cross
            inv[q] = 1.0 / piv[q][q]
            inv[q + 1] = piv[q][q] * (1.0 / minor)
            mult[q][q + 1] = cross * inv[q]
            piv[q + 1][q + 1] = minor * inv[q]
            for r in range(q + 2, 8):
                mult[q][r] = piv[q][r] * inv[q]
                piv[q + 1][r] = piv[q + 1][r] - mult[q][q + 1] * piv[q][r]
                mult[q + 1][r] = piv[q + 1][r] * inv[q + 1]
            for r in range(q + 2, 8):
                for s in range(r, 8):
                    piv[r][s] = (piv[r][s] - mult[q][r] * piv[q][s]) - mult[q + 1][r] * piv[q + 1][s]
        for q in range(8):
            scale = piv[q][q] if scale is None else jnp.where(sub == q, piv[q][q], scale)
        root = lax.rsqrt(scale)
        scale = root * (1.5 - 0.5 * scale * root * root)
        scales.append(scale)
        rows = []
        for q in range(8):
            row = jnp.broadcast_to(own[q:q + 1, :], wide)
            row = jnp.where(lane == base + q, inv[q], row * inv[q])
            rows.append(row)
            masked = jnp.where(sub > q, cols[q], 0.0)
            own = jnp.where((lane == base + q) & (sub > q), 0.0, own) - masked * row
            for r in range(q + 1, 8):
                cols[r] = cols[r] - masked * mult[q][r]
        block[t] = own
        if t + 1 == groups:
            continue
        cur = block[t + 1]
        coef = [jnp.broadcast_to(cur[:, base + q:base + q + 1], wide) for q in range(8)]
        for q in range(8):
            cur = jnp.where(lane == base + q, 0.0, cur) - coef[q] * rows[q]
            for r in range(q + 1, 8):
                coef[r] = coef[r] - coef[q] * mult[q][r]
        block[t + 1] = cur
        if t + 2 == groups:
            continue
        panel = (lane >= base) & (lane < base + 8)
        rows = [jnp.where((lane > base + q) & (lane < base + 8), 0.0, rows[q]) for q in range(8)]
        right = rows[0]
        for q in range(1, 8):
            right = jnp.where(sub == q, rows[q], right)
        ah, am, al = split3(own)
        bh, bm, bl = split3(right)
        upd = lax.dot_general(jnp.concatenate([ah, ah, am, ah, al, am], axis=0),
                              jnp.concatenate([bh, bm, bh, bl, bh, bm], axis=0),
                              (((0,), (0,)), ((), ())), preferred_element_type=jnp.float32)
        for s in range(t + 2, groups):
            block[s] = jnp.where(panel, 0.0, block[s]) - upd[8 * s:8 * s + 8, :]
    for t in range(groups):
        diff = lane - sub - 8 * t
        block[t] = scales[t] * jnp.where(diff < 0, block[t], jnp.where(diff == 0, 1.0, 0.0))
    return block


def stack_left(value, axis):
    high, mid, low = split3(value)
    return jnp.concatenate([high, high, mid, high, low, mid], axis=axis)


def stack_right(value, axis):
    high, mid, low = split3(value)
    return jnp.concatenate([high, mid, high, low, high, mid], axis=axis)


def mm(a, b):
    return lax.dot_general(a, b, (((1,), (0,)), ((), ())), preferred_element_type=jnp.float32)


def kernel(row_total, x_ref, ids_ref, out_ref,
           part, got_c, half, got_y, quarter, got_z, mom, flat,
           stage, send_rows, between, got, work, diag, left, right, white, rows,
           ret, ret_between, ret_got,
           c_send, c_recv, y_send, y_recv, z_send, z_recv,
           gz_send, gz_recv, a_send, a_recv, b_send, b_recv,
           a2_send, a2_recv, b2_send, b2_recv, gc_send, gc_recv,
           d_send, d_recv, e_send, e_recv, x_send, x_recv,
           r_send, r_recv, t_send, t_recv):
    f32, bf16 = jnp.float32, jnp.bfloat16
    m = lax.axis_index("mp")
    d = lax.axis_index("dp")
    c = lax.rem(d, 2)
    z = lax.rem(lax.div(d, 2), NZ)
    y = lax.div(d, 2 * NZ)

    def dev(yy, zz, cc, mm):
        return ((yy * NZ + zz) * 2 + cc, mm)

    sibling = dev(y, z, 1 - c, m)
    y_peers = [lax.rem(y + o, NY) for o in (2, 1, 3)]
    z_peers = [lax.rem(z + o, NZ) for o in (8, 7, 9, 6, 10, 5, 11, 4, 12, 3, 13, 2, 14, 1, 15)]
    x_peers = [lax.rem(m + o, NX) for o in (2, 1, 3)]
    plane = [(lax.rem(y + o, NY), co) for o in (2, 1, 3) for co in (1 - c, c)] + [(y, 1 - c)]
    barrier = pltpu.get_barrier_semaphore()
    everyone = ([dev(y, p, c, m) for p in z_peers] + [dev(yy, z, co, m) for yy, co in plane]
                + [dev(y, z, c, p) for p in x_peers])
    for peer in everyone:
        pl.semaphore_signal(barrier, inc=1, device_id=peer, device_id_type=MESH)

    for i in range(NB):
        j = lax.rem(i + m, NB)
        lhs = x_ref[:, i * BLK:(i + 1) * BLK]
        rhs = x_ref[:, pl.ds(pl.multiple_of(j * BLK, BLK), BLK)]
        prod = lax.dot_general(lhs, rhs, (((0,), (0,)), ((), ())),
                               preferred_element_type=f32)
        part[:, :, :, i, :] = prod.reshape(NC, NY, NZ, BLK)

    count = x_ref.shape[0]
    owner = lax.div(ids_ref[...], CPO)
    within = (ids_ref[...] - owner * CPO + 1).astype(f32)
    owner = owner.astype(f32)
    owner_row = jnp.broadcast_to(owner, (count, count))
    first = lax.broadcasted_iota(jnp.int32, (count, count), 0)
    second = lax.broadcasted_iota(jnp.int32, (count, count), 1)
    earlier = (owner_row == owner_row.T) & (first < second)
    rank = jnp.sum(jnp.where(earlier, 1.0, 0.0), axis=0, keepdims=True)
    owner_iota = lax.broadcasted_iota(jnp.int32, (N_DP, count), 0).astype(f32)
    pick = jnp.where((owner_iota == owner) & (rank == m.astype(f32)), 1.0, 0.0)
    picked = lax.dot_general(pick.astype(bf16), x_ref[...], (((1,), (0,)), ((), ())),
                             preferred_element_type=f32)
    label = jnp.sum(pick * within, axis=1, keepdims=True) - 1.0
    for i in range(NB):
        stage[pl.ds(i, N_DP, stride=NB + 2), :] = picked[:, i * BLK:(i + 1) * BLK]
    stage[pl.ds(NB, N_DP, stride=NB + 2), :] = jnp.broadcast_to(label, (N_DP, BLK))
    stage[pl.ds(NB + 1, N_DP, stride=NB + 2), :] = jnp.zeros((N_DP, BLK), f32)
    send_rows[...] = stage[...].reshape(NY, NZ, NC, NB + 2, BLK).astype(bf16)
    between[y, c] = send_rows[y, :, c]
    pl.semaphore_wait(barrier, len(everyone))

    def copy(src, dst, send, recv, device):
        return pltpu.make_async_remote_copy(
            src_ref=src, dst_ref=dst, send_sem=send, recv_sem=recv,
            device_id=device, device_id_type=MESH)

    cc = copy(part.at[1 - c], got_c, c_send, c_recv, sibling)
    cc.start()
    cc.wait_recv()
    half[...] = part[c] + got_c[...]
    sent = []
    for p in y_peers:
        cp = copy(half.at[p], got_y.at[y], y_send.at[p], y_recv.at[y], dev(p, z, c, m))
        cp.start()
        sent.append(cp)
    total = half[y]
    for p in y_peers:
        copy(half.at[p], got_y.at[p], y_send.at[p], y_recv.at[p], dev(p, z, c, m)).wait_recv()
        total = total + got_y[p]
    quarter[...] = total
    for p in z_peers:
        cp = copy(quarter.at[p], got_z.at[z], z_send.at[p], z_recv.at[z], dev(y, p, c, m))
        cp.start()
        sent.append(cp)
    for yy, co in plane:
        cp = copy(send_rows.at[yy, :, co], between.at[y, c], d_send.at[yy * NC + co],
                  d_recv.at[y * NC + c], dev(yy, z, co, m))
        cp.start()
        sent.append(cp)
    row = quarter[z]
    for p in reversed(z_peers):
        copy(quarter.at[p], got_z.at[p], z_send.at[p], z_recv.at[p], dev(y, p, c, m)).wait_recv()
        row = row + got_z[p]
    mom[m, c, y, z] = row
    for p in z_peers:
        cp = copy(mom.at[m, c, y, z], mom.at[m, c, y, z], gz_send.at[p], gz_recv.at[z],
                  dev(y, p, c, m))
        cp.start()
        sent.append(cp)

    for p in reversed(z_peers):
        copy(mom.at[m, c, y, p], mom.at[m, c, y, p], gz_send.at[p], gz_recv.at[p],
             dev(y, p, c, m)).wait_recv()
    for yy, co in plane:
        copy(send_rows.at[yy, :, co], between.at[yy, co], d_send.at[yy * NC + co],
             d_recv.at[yy * NC + co], dev(yy, z, co, m)).wait_recv()
    late = []
    for p in z_peers:
        cp = copy(between.at[:, :, p], got.at[m, :, :, z], e_send.at[p], e_recv.at[z],
                  dev(y, p, c, m))
        cp.start()
        late.append(cp)
    got[m, :, :, z] = between[:, :, z]
    lo, hi = pl.ds(0, NZ // 2), pl.ds(NZ // 2, NZ // 2)

    def piece(n, core):
        kind, peer = divmod(n + 2, 3)
        return (mom.at[m, core, y],
                mom.at[m, core, y_peers[peer], lo],
                mom.at[x_peers[peer], core, y, hi],
                mom.at[x_peers[peer], core, :, lo],
                mom.at[:, core, y_peers[peer], hi])[kind]

    def pass_on(n):
        cp = copy(piece(n, c), piece(n, c), gc_send.at[n], gc_recv.at[n], sibling)
        cp.start()
        sent.append(cp)

    pass_on(0)
    for p in y_peers:
        cp = copy(mom.at[m, c, y, lo], mom.at[m, c, y, lo], a_send.at[p], a_recv.at[y],
                  dev(p, z, c, m))
        cp.start()
        sent.append(cp)
    for p in x_peers:
        cp = copy(mom.at[m, c, y, hi], mom.at[m, c, y, hi], b_send.at[p], b_recv.at[m],
                  dev(y, z, c, p))
        cp.start()
        sent.append(cp)
    for n, p in enumerate(y_peers):
        copy(mom.at[m, c, p, lo], mom.at[m, c, p, lo], a_send.at[p], a_recv.at[p],
             dev(p, z, c, m)).wait_recv()
        pass_on(1 + n)
    for p in x_peers:
        cp = copy(mom.at[m, c, :, lo], mom.at[m, c, :, lo], a2_send.at[p], a2_recv.at[m],
                  dev(y, z, c, p))
        cp.start()
        sent.append(cp)
    for n, p in enumerate(x_peers):
        copy(mom.at[p, c, y, hi], mom.at[p, c, y, hi], b_send.at[p], b_recv.at[p],
             dev(y, z, c, p)).wait_recv()
        pass_on(4 + n)
    for p in y_peers:
        cp = copy(mom.at[:, c, y, hi], mom.at[:, c, y, hi], b2_send.at[p], b2_recv.at[y],
                  dev(p, z, c, m))
        cp.start()
        sent.append(cp)
    for n, p in enumerate(x_peers):
        copy(mom.at[p, c, :, lo], mom.at[p, c, :, lo], a2_send.at[p], a2_recv.at[p],
             dev(y, z, c, p)).wait_recv()
        pass_on(7 + n)
    for n, p in enumerate(y_peers):
        copy(mom.at[:, c, p, hi], mom.at[:, c, p, hi], b2_send.at[p], b2_recv.at[p],
             dev(p, z, c, m)).wait_recv()
        pass_on(10 + n)
    for n in range(13):
        copy(piece(n, 1 - c), piece(n, 1 - c), gc_send.at[n], gc_recv.at[n], sibling).wait_recv()
    cc.wait_send()
    for cp in sent:
        cp.wait_send()

    for i in range(0, NB, 2):
        white[i * BLK:(i + 1) * BLK, (i + 1) * BLK:(i + 2) * BLK] = jnp.zeros((BLK, BLK), bf16)
    scale = 1.0 / row_total
    eye = jnp.where(lax.broadcasted_iota(jnp.int32, (BLK, BLK), 0)
                    == lax.broadcasted_iota(jnp.int32, (BLK, BLK), 1), 0.001, 0.0)

    def at(i, j):
        return (slice(i * BLK, (i + 1) * BLK), slice(j * BLK, (j + 1) * BLK))

    def moment_block(g, i):
        return flat[pl.ds(g * N_DP * 8 + i, N_DP, stride=8), :] * scale

    @pl.loop(0, NX * N_DP // 16)
    def _(b):
        for r in range(16):
            flat[pl.ds(pl.multiple_of(b * BLK, BLK) + 8 * r, NB), :] = (
                mom[lax.div(b, 8), lax.div(lax.rem(b, 8), 4), lax.rem(b, 4), r])

    for i in range(NB):
        for g in range(4):
            j = i + g
            if j < NB:
                val = moment_block(g, i)
                work[at(i, j)] = val + eye if g == 0 else val
            elif g < 3:
                work[at(j - NB, i)] = moment_block(g, i).T

    @pl.loop(0, NB)
    def _(k):
        for kk in range(NB):
            @pl.when(k == kk)
            def _():
                diag[...] = work[at(kk, kk)]
                if kk == GATHER_AT:
                    for p in z_peers:
                        copy(between.at[:, :, p], got.at[m, :, :, p], e_send.at[p], e_recv.at[p],
                             dev(y, p, c, m)).wait_recv()
                    for p in x_peers:
                        copy(got.at[m], got.at[m], x_send.at[p], x_recv.at[m],
                             (d, p)).start()
        block = lower_inverse([diag[8 * t:8 * t + 8, :] for t in range(BLK // 8)])
        for t in range(BLK // 8):
            diag[8 * t:8 * t + 8, :] = block[t]
        for kk in range(NB):
            @pl.when(k == kk)
            def _():
                rk = slice(kk * BLK, (kk + 1) * BLK)
                inverse = diag[...]
                line = mm(stack_left(inverse, 1), stack_right(work[rk, :], 0))
                white[at(kk, kk)] = inverse.astype(bf16)
                if kk:
                    white[rk, :kk * BLK] = line[:, :kk * BLK].astype(bf16)
                if kk == NB - 1:
                    return
                done = (kk + 1) * BLK
                left[done:, :] = stack_left(line[:, done:].T, 1)
                right[:, :kk * BLK + BLK] = stack_right(
                    jnp.concatenate([line[:, :kk * BLK], inverse], axis=1) if kk else inverse, 0)
                right[:, done:] = stack_right(line[:, done:], 0)
                old = mm(left[done:, :], right[:, :done])
                if kk:
                    work[done:, :kk * BLK] = work[done:, :kk * BLK] - old[:, :kk * BLK]
                work[done:, rk] = -old[:, rk]
                for i in range(kk + 1, NB, 2):
                    ri = slice(i * BLK, min(i + 2, NB) * BLK)
                    work[ri, i * BLK:] = work[ri, i * BLK:] - mm(left[ri, :], right[:, i * BLK:])

    for p in x_peers:
        copy(got.at[p], got.at[p], x_send.at[p], x_recv.at[p], (d, p)).wait()
    for cp in late:
        cp.wait_send()
    labels = []
    for k in range(PAIR):
        stage[...] = got[k].astype(f32).reshape(N_DP * (NB + 2), BLK)
        for i in range(NB):
            rows[k * N_DP:(k + 1) * N_DP, i * BLK:(i + 1) * BLK] = (
                stage[pl.ds(i, N_DP, stride=NB + 2), :].astype(bf16))
        labels.append(stage[pl.ds(NB, N_DP, stride=NB + 2), :])
    wide = 2 * BLK
    whitened = jnp.concatenate(
        [lax.dot_general(rows[:, :n + wide], white[n:n + wide, :n + wide],
                         (((1,), (1,)), ((), ())), preferred_element_type=f32)
         for n in range(0, D, wide)], axis=1).astype(bf16)
    widened = whitened.astype(f32)
    square_sum = jnp.sum(widened * widened, axis=1, keepdims=True)
    rows[...] = (widened * lax.rsqrt(square_sum + 1e-06)).astype(bf16)
    lane = lax.broadcasted_iota(jnp.int32, (N_DP, N_DP), 1)
    other = lax.broadcasted_iota(jnp.int32, (N_DP, N_DP), 0) != lane
    flipped = [value.T for value in labels]
    reply = jnp.zeros((N_DP, N_DP), f32)
    for a in range(PAIR):
        sim = lax.dot_general(rows[a * N_DP:(a + 1) * N_DP, :], rows[...],
                              (((1,), (1,)), ((), ())), preferred_element_type=f32)
        best = jnp.full((N_DP, N_DP), -1.0, f32)
        for b in range(PAIR):
            same = (labels[a] == flipped[b]) & (labels[a] >= 0.0)
            if a == b:
                same = same & other
            best = jnp.maximum(best, jnp.where(same, sim[:, b * N_DP:(b + 1) * N_DP], -1.0))
        reply = jnp.where(lane == a, jnp.max(best, axis=1, keepdims=True), reply)
    ret[:, :, :, 0, :] = reply.reshape(NY, NC, NZ, BLK)
    back = []
    for p in z_peers:
        cp = copy(ret.at[:, :, p], ret_between.at[z], r_send.at[p], r_recv.at[z], dev(y, p, c, m))
        cp.start()
        back.append(cp)
    ret_between[z] = ret[:, :, z]
    for p in reversed(z_peers):
        copy(ret.at[:, :, p], ret_between.at[p], r_send.at[p], r_recv.at[p],
             dev(y, p, c, m)).wait_recv()
    for yy, co in plane:
        cp = copy(ret_between.at[:, yy, co], ret_got.at[y, c], t_send.at[yy * NC + co],
                  t_recv.at[y * NC + c], dev(yy, z, co, m))
        cp.start()
        back.append(cp)
    ret_got[y, c] = ret_between[:, y, c]
    spot = lax.broadcasted_iota(jnp.int32, (N_DP, count), 0)
    spot_z, spot_yc = lax.rem(spot, NZ), lax.div(spot, NZ)
    spot = (lax.div(spot_yc, NC) * NZ + spot_z) * NC + lax.rem(spot_yc, NC)
    hit = jnp.where(spot.astype(f32) == owner, 1.0, 0.0)
    for yy, co in plane:
        copy(ret_between.at[:, yy, co], ret_got.at[yy, co], t_send.at[yy * NC + co],
             t_recv.at[yy * NC + co], dev(yy, z, co, m)).wait_recv()
    for cp in back:
        cp.wait_send()
    table = lax.dot_general(ret_got[:, :, :, 0, :].reshape(N_DP, BLK), hit,
                            (((0,), (0,)), ((), ())), precision=HIGH, preferred_element_type=f32)
    score = jnp.zeros((1, count), f32)
    for k in range(PAIR):
        score = jnp.where(rank == float(k), table[k:k + 1, :], score)
    out_ref[...] = score


def local(embeddings, cluster_ids):
    row_count, feat_width = embeddings.shape
    dp_count = lax.axis_size("dp")
    f32, bf16 = jnp.float32, jnp.bfloat16
    dma = pltpu.SemaphoreType.DMA
    scratch = [
        pltpu.VMEM((NC, NY, NZ, NB, BLK), f32),
        pltpu.VMEM((NY, NZ, NB, BLK), f32),
        pltpu.VMEM((NY, NZ, NB, BLK), f32),
        pltpu.VMEM((NY, NZ, NB, BLK), f32),
        pltpu.VMEM((NZ, NB, BLK), f32),
        pltpu.VMEM((NZ, NB, BLK), f32),
        pltpu.VMEM((NX, NC, NY, NZ, NB, BLK), f32),
        pltpu.VMEM((NX * N_DP * 8, BLK), f32),
        pltpu.VMEM((N_DP * (NB + 2), BLK), f32),
        pltpu.VMEM((NY, NZ, NC, NB + 2, BLK), bf16),
        pltpu.VMEM((NY, NC, NZ, NB + 2, BLK), bf16),
        pltpu.VMEM((NX, NY, NC, NZ, NB + 2, BLK), bf16),
        pltpu.VMEM((D, D), f32),
        pltpu.VMEM((BLK, BLK), f32),
        pltpu.VMEM((D, 6 * BLK), bf16),
        pltpu.VMEM((6 * BLK, D), bf16),
        pltpu.VMEM((D, D), bf16),
        pltpu.VMEM((PAIR * N_DP, D), bf16),
        pltpu.VMEM((NY, NC, NZ, 1, BLK), f32),
        pltpu.VMEM((NZ, NY, NC, 1, BLK), f32),
        pltpu.VMEM((NY, NC, NZ, 1, BLK), f32),
        dma, dma, dma((NY,)), dma((NY,)), dma((NZ,)), dma((NZ,)),
        dma((NZ,)), dma((NZ,)), dma((NY,)), dma((NY,)), dma((NX,)), dma((NX,)),
        dma((NX,)), dma((NX,)), dma((NY,)), dma((NY,)), dma((13,)), dma((13,)),
        dma((NY * NC,)), dma((NY * NC,)), dma((NZ,)), dma((NZ,)), dma((NX,)), dma((NX,)),
        dma((NZ,)), dma((NZ,)), dma((NY * NC,)), dma((NY * NC,)),
    ]
    vm = pl.BlockSpec(memory_space=pltpu.VMEM)
    scores = pl.pallas_call(
        functools.partial(kernel, float(row_count * dp_count)),
        out_shape=jax.ShapeDtypeStruct((1, row_count), f32),
        in_specs=[vm, vm],
        out_specs=vm,
        scratch_shapes=scratch,
        name="dedup",
        compiler_params=pltpu.CompilerParams(collective_id=0, has_side_effects=True),
    )(embeddings, cluster_ids.reshape(1, row_count))
    return scores.reshape(row_count)


def solution(mesh):
    in_specs = (P("dp", None), P("dp"))
    out_specs = P("dp")
    return jax.shard_map(local, mesh=mesh, in_specs=in_specs, out_specs=out_specs, check_vma=False)
```

```python
import functools

import jax
import jax.numpy as jnp
from jax import lax
from jax.experimental import pallas as pl
from jax.experimental.pallas import tpu as pltpu
from jax.sharding import PartitionSpec as P

CPO = 4
NX, NC, NY, NZ = 4, 2, 4, 16
BLK = 128
NB = 6
D = NB * BLK
N_DP = NC * NY * NZ
PAIR = 4
GATHER_AT = 1
RELAY_AT = 3
MESH = pl.DeviceIdType.MESH
HIGH = lax.Precision.HIGHEST


def split3(value):
    high = value.astype(jnp.bfloat16)
    rest = value - high.astype(jnp.float32)
    mid = rest.astype(jnp.bfloat16)
    low = (rest - mid.astype(jnp.float32)).astype(jnp.bfloat16)
    return high, mid, low


def lower_inverse(block):
    lane = lax.broadcasted_iota(jnp.int32, (8, BLK), 1)
    sub = lax.broadcasted_iota(jnp.int32, (8, BLK), 0)
    groups = BLK // 8
    wide = (8, BLK)
    picks = [jnp.full(wide, q, jnp.int32) for q in range(8)]
    scales = []
    for t in range(groups):
        own = block[t]
        base = 8 * t
        cols = [jnp.broadcast_to(own[:, base + q:base + q + 1], wide) for q in range(8)]
        piv = [[None] * 8 for _ in range(8)]
        for q in range(8):
            for r in range(q, 8):
                piv[q][r] = jnp.take_along_axis(cols[r], picks[q], axis=0)
        mult = [[None] * 8 for _ in range(8)]
        inv = [None] * 8
        scale = None
        for q in range(0, 8, 2):
            cross, last = piv[q][q + 1], piv[q + 1][q + 1]
            minor = piv[q][q] * last - cross * cross
            inv[q] = 1.0 / piv[q][q]
            inv[q + 1] = piv[q][q] * (1.0 / minor)
            mult[q][q + 1] = cross * inv[q]
            piv[q + 1][q + 1] = minor * inv[q]
            for r in range(q + 2, 8):
                mult[q][r] = piv[q][r] * inv[q]
                piv[q + 1][r] = piv[q + 1][r] - mult[q][q + 1] * piv[q][r]
                mult[q + 1][r] = piv[q + 1][r] * inv[q + 1]
            for r in range(q + 2, 8):
                for s in range(r, 8):
                    piv[r][s] = (piv[r][s] - mult[q][r] * piv[q][s]) - mult[q + 1][r] * piv[q + 1][s]
        for q in range(8):
            scale = piv[q][q] if scale is None else jnp.where(sub == q, piv[q][q], scale)
        root = lax.rsqrt(scale)
        scale = root * (1.5 - 0.5 * scale * root * root)
        scales.append(scale)
        rows = []
        for q in range(8):
            row = jnp.broadcast_to(own[q:q + 1, :], wide)
            row = jnp.where(lane == base + q, inv[q], row * inv[q])
            rows.append(row)
            masked = jnp.where(sub > q, cols[q], 0.0)
            own = jnp.where((lane == base + q) & (sub > q), 0.0, own) - masked * row
            for r in range(q + 1, 8):
                cols[r] = cols[r] - masked * mult[q][r]
        block[t] = own
        if t + 1 == groups:
            continue
        cur = block[t + 1]
        coef = [jnp.broadcast_to(cur[:, base + q:base + q + 1], wide) for q in range(8)]
        for q in range(8):
            cur = jnp.where(lane == base + q, 0.0, cur) - coef[q] * rows[q]
            for r in range(q + 1, 8):
                coef[r] = coef[r] - coef[q] * mult[q][r]
        block[t + 1] = cur
        if t + 2 == groups:
            continue
        panel = (lane >= base) & (lane < base + 8)
        rows = [jnp.where((lane > base + q) & (lane < base + 8), 0.0, rows[q]) for q in range(8)]
        right = rows[0]
        for q in range(1, 8):
            right = jnp.where(sub == q, rows[q], right)
        ah, am, al = split3(own)
        bh, bm, bl = split3(right)
        upd = lax.dot_general(jnp.concatenate([ah, ah, am, ah, al, am], axis=0),
                              jnp.concatenate([bh, bm, bh, bl, bh, bm], axis=0),
                              (((0,), (0,)), ((), ())), preferred_element_type=jnp.float32)
        for s in range(t + 2, groups):
            block[s] = jnp.where(panel, 0.0, block[s]) - upd[8 * s:8 * s + 8, :]
    for t in range(groups):
        diff = lane - sub - 8 * t
        block[t] = scales[t] * jnp.where(diff < 0, block[t], jnp.where(diff == 0, 1.0, 0.0))
    return block


def stack_left(value, axis):
    high, mid, low = split3(value)
    return jnp.concatenate([high, high, mid, high, low, mid], axis=axis)


def stack_right(value, axis):
    high, mid, low = split3(value)
    return jnp.concatenate([high, mid, high, low, high, mid], axis=axis)


def mm(a, b):
    return lax.dot_general(a, b, (((1,), (0,)), ((), ())), preferred_element_type=jnp.float32)


def kernel(row_total, x_ref, ids_ref, out_ref,
           part, got_c, half, got_y, quarter, got_z, mom, flat,
           stage, send_rows, between, got, work, left, right, white, rows,
           ret, ret_between, ret_got,
           c_send, c_recv, y_send, y_recv, z_send, z_recv,
           gz_send, gz_recv, a_send, a_recv, b_send, b_recv,
           a2_send, a2_recv, b2_send, b2_recv, gc_send, gc_recv,
           d_send, d_recv, e_send, e_recv, x_send, x_recv, f_send, f_recv,
           r_send, r_recv, t_send, t_recv):
    f32, bf16 = jnp.float32, jnp.bfloat16
    m = lax.axis_index("mp")
    d = lax.axis_index("dp")
    c = lax.rem(d, 2)
    z = lax.rem(lax.div(d, 2), NZ)
    y = lax.div(d, 2 * NZ)

    def dev(yy, zz, cc, mm):
        return ((yy * NZ + zz) * 2 + cc, mm)

    sibling = dev(y, z, 1 - c, m)
    y_peers = [lax.rem(y + o, NY) for o in (2, 1, 3)]
    z_peers = [lax.rem(z + o, NZ) for o in (8, 7, 9, 6, 10, 5, 11, 4, 12, 3, 13, 2, 14, 1, 15)]
    x_peers = [lax.rem(m + o, NX) for o in (2, 1, 3)]
    plane = [(lax.rem(y + o, NY), co) for o in (2, 1, 3) for co in (1 - c, c)] + [(y, 1 - c)]
    barrier = pltpu.get_barrier_semaphore()
    everyone = ([dev(y, p, c, m) for p in z_peers] + [dev(yy, z, co, m) for yy, co in plane]
                + [dev(y, z, c, p) for p in x_peers])
    for peer in everyone:
        pl.semaphore_signal(barrier, inc=1, device_id=peer, device_id_type=MESH)

    for i in range(NB):
        j = lax.rem(i + m, NB)
        lhs = x_ref[:, i * BLK:(i + 1) * BLK]
        rhs = x_ref[:, pl.ds(pl.multiple_of(j * BLK, BLK), BLK)]
        prod = lax.dot_general(lhs, rhs, (((0,), (0,)), ((), ())),
                               preferred_element_type=f32)
        part[:, :, :, i, :] = prod.reshape(NC, NY, NZ, BLK)

    count = x_ref.shape[0]
    owner = lax.div(ids_ref[...], CPO)
    within = (ids_ref[...] - owner * CPO + 1).astype(f32)
    owner = owner.astype(f32)
    owner_row = jnp.broadcast_to(owner, (count, count))
    first = lax.broadcasted_iota(jnp.int32, (count, count), 0)
    second = lax.broadcasted_iota(jnp.int32, (count, count), 1)
    earlier = (owner_row == owner_row.T) & (first < second)
    rank = jnp.sum(jnp.where(earlier, 1.0, 0.0), axis=0, keepdims=True)
    owner_iota = lax.broadcasted_iota(jnp.int32, (N_DP, count), 0).astype(f32)
    pick = jnp.where((owner_iota == owner) & (rank == m.astype(f32)), 1.0, 0.0)
    picked = lax.dot_general(pick.astype(bf16), x_ref[...], (((1,), (0,)), ((), ())),
                             preferred_element_type=f32)
    label = jnp.sum(pick * within, axis=1, keepdims=True) - 1.0
    for i in range(NB):
        stage[pl.ds(i, N_DP, stride=NB + 2), :] = picked[:, i * BLK:(i + 1) * BLK]
    stage[pl.ds(NB, N_DP, stride=NB + 2), :] = jnp.broadcast_to(label, (N_DP, BLK))
    stage[pl.ds(NB + 1, N_DP, stride=NB + 2), :] = jnp.zeros((N_DP, BLK), f32)
    send_rows[...] = stage[...].reshape(NY, NZ, NC, NB + 2, BLK).astype(bf16)
    between[y, c] = send_rows[y, :, c]
    pl.semaphore_wait(barrier, len(everyone))

    def copy(src, dst, send, recv, device):
        return pltpu.make_async_remote_copy(
            src_ref=src, dst_ref=dst, send_sem=send, recv_sem=recv,
            device_id=device, device_id_type=MESH)

    cc = copy(part.at[1 - c], got_c, c_send, c_recv, sibling)
    cc.start()
    cc.wait_recv()
    half[...] = part[c] + got_c[...]
    sent = []
    for p in y_peers:
        cp = copy(half.at[p], got_y.at[y], y_send.at[p], y_recv.at[y], dev(p, z, c, m))
        cp.start()
        sent.append(cp)
    total = half[y]
    for p in y_peers:
        copy(half.at[p], got_y.at[p], y_send.at[p], y_recv.at[p], dev(p, z, c, m)).wait_recv()
        total = total + got_y[p]
    quarter[...] = total
    for p in z_peers:
        cp = copy(quarter.at[p], got_z.at[z], z_send.at[p], z_recv.at[z], dev(y, p, c, m))
        cp.start()
        sent.append(cp)
    for yy, co in plane:
        cp = copy(send_rows.at[yy, :, co], between.at[y, c], d_send.at[yy * NC + co],
                  d_recv.at[y * NC + c], dev(yy, z, co, m))
        cp.start()
        sent.append(cp)
    row = quarter[z]
    for p in reversed(z_peers):
        copy(quarter.at[p], got_z.at[p], z_send.at[p], z_recv.at[p], dev(y, p, c, m)).wait_recv()
        row = row + got_z[p]
    mom[m, c, y, z] = row
    for p in z_peers:
        cp = copy(mom.at[m, c, y, z], mom.at[m, c, y, z], gz_send.at[p], gz_recv.at[z],
                  dev(y, p, c, m))
        cp.start()
        sent.append(cp)

    for p in reversed(z_peers):
        copy(mom.at[m, c, y, p], mom.at[m, c, y, p], gz_send.at[p], gz_recv.at[p],
             dev(y, p, c, m)).wait_recv()
    for yy, co in plane:
        copy(send_rows.at[yy, :, co], between.at[yy, co], d_send.at[yy * NC + co],
             d_recv.at[yy * NC + co], dev(yy, z, co, m)).wait_recv()
    late = []
    for p in z_peers:
        cp = copy(between.at[:, :, p], got.at[m, :, :, z], e_send.at[p], e_recv.at[z],
                  dev(y, p, c, m))
        cp.start()
        late.append(cp)
    got[m, :, :, z] = between[:, :, z]
    lo, hi = pl.ds(0, NZ // 2), pl.ds(NZ // 2, NZ // 2)

    def piece(n, core):
        kind, peer = divmod(n + 2, 3)
        return (mom.at[m, core, y],
                mom.at[m, core, y_peers[peer], lo],
                mom.at[x_peers[peer], core, y, hi],
                mom.at[x_peers[peer], core, :, lo],
                mom.at[:, core, y_peers[peer], hi])[kind]

    def pass_on(n):
        cp = copy(piece(n, c), piece(n, c), gc_send.at[n], gc_recv.at[n], sibling)
        cp.start()
        sent.append(cp)

    pass_on(0)
    for p in y_peers:
        cp = copy(mom.at[m, c, y, lo], mom.at[m, c, y, lo], a_send.at[p], a_recv.at[y],
                  dev(p, z, c, m))
        cp.start()
        sent.append(cp)
    for p in x_peers:
        cp = copy(mom.at[m, c, y, hi], mom.at[m, c, y, hi], b_send.at[p], b_recv.at[m],
                  dev(y, z, c, p))
        cp.start()
        sent.append(cp)
    for n, p in enumerate(y_peers):
        copy(mom.at[m, c, p, lo], mom.at[m, c, p, lo], a_send.at[p], a_recv.at[p],
             dev(p, z, c, m)).wait_recv()
        pass_on(1 + n)
    for p in x_peers:
        cp = copy(mom.at[m, c, :, lo], mom.at[m, c, :, lo], a2_send.at[p], a2_recv.at[m],
                  dev(y, z, c, p))
        cp.start()
        sent.append(cp)
    for n, p in enumerate(x_peers):
        copy(mom.at[p, c, y, hi], mom.at[p, c, y, hi], b_send.at[p], b_recv.at[p],
             dev(y, z, c, p)).wait_recv()
        pass_on(4 + n)
    for p in y_peers:
        cp = copy(mom.at[:, c, y, hi], mom.at[:, c, y, hi], b2_send.at[p], b2_recv.at[y],
                  dev(p, z, c, m))
        cp.start()
        sent.append(cp)
    for n, p in enumerate(x_peers):
        copy(mom.at[p, c, :, lo], mom.at[p, c, :, lo], a2_send.at[p], a2_recv.at[p],
             dev(y, z, c, p)).wait_recv()
        pass_on(7 + n)
    for n, p in enumerate(y_peers):
        copy(mom.at[:, c, p, hi], mom.at[:, c, p, hi], b2_send.at[p], b2_recv.at[p],
             dev(p, z, c, m)).wait_recv()
        pass_on(10 + n)
    for n in range(13):
        copy(piece(n, 1 - c), piece(n, 1 - c), gc_send.at[n], gc_recv.at[n], sibling).wait_recv()
    cc.wait_send()
    for cp in sent:
        cp.wait_send()

    for i in range(0, NB, 2):
        white[i * BLK:(i + 1) * BLK, (i + 1) * BLK:(i + 2) * BLK] = jnp.zeros((BLK, BLK), bf16)
    scale = 1.0 / row_total
    eye = jnp.where(lax.broadcasted_iota(jnp.int32, (BLK, BLK), 0)
                    == lax.broadcasted_iota(jnp.int32, (BLK, BLK), 1), 0.001, 0.0)

    def at(i, j):
        return (slice(i * BLK, (i + 1) * BLK), slice(j * BLK, (j + 1) * BLK))

    def moment_block(g, i):
        return flat[pl.ds(g * N_DP * 8 + i, N_DP, stride=8), :] * scale

    @pl.loop(0, NX * N_DP // 16)
    def _(b):
        for r in range(16):
            flat[pl.ds(pl.multiple_of(b * BLK, BLK) + 8 * r, NB), :] = (
                mom[lax.div(b, 8), lax.div(lax.rem(b, 8), 4), lax.rem(b, 4), r])

    for i in range(NB):
        for g in range(4):
            j = i + g
            if j < NB:
                val = moment_block(g, i)
                work[at(i, j)] = val + eye if g == 0 else val
            elif g < 3:
                work[at(j - NB, i)] = moment_block(g, i).T

    labels = []
    following, previous, opposite = (lax.rem(m + o, NX) for o in (1, 3, 2))
    halves = (pl.ds(0, NY // 2), pl.ds(NY // 2, NY // 2))
    corner = work[at(0, 0)]
    for kk in range(NB):
        if kk == GATHER_AT:
            for p in z_peers:
                copy(between.at[:, :, p], got.at[m, :, :, p], e_send.at[p], e_recv.at[p],
                     dev(y, p, c, m)).wait_recv()
            for p in (following, previous):
                cp = copy(got.at[m], got.at[m], x_send.at[p], x_recv.at[m], (d, p))
                cp.start()
                late.append(cp)
        if kk == RELAY_AT:
            for p in (following, previous):
                copy(got.at[p], got.at[p], x_send.at[p], x_recv.at[p], (d, p)).wait_recv()
            for n, (source, p) in enumerate(((previous, following), (following, previous))):
                part_of = got.at[source, halves[n]]
                cp = copy(part_of, part_of, f_send.at[n], f_recv.at[n], (d, p))
                cp.start()
                late.append(cp)
        if kk == NB - 1:
            for n, p in enumerate((previous, following)):
                part_of = got.at[opposite, halves[n]]
                copy(part_of, part_of, f_send.at[n], f_recv.at[n], (d, p)).wait_recv()
            for k in range(PAIR):
                stage[...] = got[k].astype(f32).reshape(N_DP * (NB + 2), BLK)
                for i in range(NB):
                    rows[k * N_DP:(k + 1) * N_DP, i * BLK:(i + 1) * BLK] = (
                        stage[pl.ds(i, N_DP, stride=NB + 2), :].astype(bf16))
                labels.append(stage[pl.ds(NB, N_DP, stride=NB + 2), :])
        inverse = jnp.concatenate(
            lower_inverse([corner[8 * t:8 * t + 8, :] for t in range(BLK // 8)]), axis=0)
        rk = slice(kk * BLK, (kk + 1) * BLK)
        line = mm(stack_left(inverse, 1), stack_right(work[rk, :], 0))
        white[at(kk, kk)] = inverse.astype(bf16)
        if kk:
            white[rk, :kk * BLK] = line[:, :kk * BLK].astype(bf16)
        if kk == NB - 1:
            break
        done = (kk + 1) * BLK
        left[done:, :] = stack_left(line[:, done:].T, 1)
        right[:, done:] = stack_right(line[:, done:], 0)
        nxt = at(kk + 1, kk + 1)
        corner = work[nxt] - mm(left[nxt[0], :], right[:, nxt[1]])
        right[:, :done] = stack_right(
            jnp.concatenate([line[:, :kk * BLK], inverse], axis=1) if kk else inverse, 0)
        old = mm(left[done:, :], right[:, :done])
        if kk:
            work[done:, :kk * BLK] = work[done:, :kk * BLK] - old[:, :kk * BLK]
        work[done:, rk] = -old[:, rk]
        for i in range(kk + 1, NB, 2):
            ri = slice(i * BLK, min(i + 2, NB) * BLK)
            work[ri, i * BLK:] = work[ri, i * BLK:] - mm(left[ri, :], right[:, i * BLK:])

    for cp in late:
        cp.wait_send()
    wide = 2 * BLK
    whitened = jnp.concatenate(
        [lax.dot_general(rows[:, :n + wide], white[n:n + wide, :n + wide],
                         (((1,), (1,)), ((), ())), preferred_element_type=f32)
         for n in range(0, D, wide)], axis=1).astype(bf16)
    widened = whitened.astype(f32)
    square_sum = jnp.sum(widened * widened, axis=1, keepdims=True)
    rows[...] = (widened * lax.rsqrt(square_sum + 1e-06)).astype(bf16)
    lane = lax.broadcasted_iota(jnp.int32, (N_DP, N_DP), 1)
    other = lax.broadcasted_iota(jnp.int32, (N_DP, N_DP), 0) != lane
    flipped = [value.T for value in labels]
    reply = jnp.zeros((N_DP, N_DP), f32)
    for a in range(PAIR):
        sim = lax.dot_general(rows[a * N_DP:(a + 1) * N_DP, :], rows[...],
                              (((1,), (1,)), ((), ())), preferred_element_type=f32)
        best = jnp.full((N_DP, N_DP), -1.0, f32)
        for b in range(PAIR):
            same = (labels[a] == flipped[b]) & (labels[a] >= 0.0)
            if a == b:
                same = same & other
            best = jnp.maximum(best, jnp.where(same, sim[:, b * N_DP:(b + 1) * N_DP], -1.0))
        reply = jnp.where(lane == a, jnp.max(best, axis=1, keepdims=True), reply)
    ret[:, :, :, 0, :] = reply.reshape(NY, NC, NZ, BLK)
    back = []
    for p in z_peers:
        cp = copy(ret.at[:, :, p], ret_between.at[z], r_send.at[p], r_recv.at[z], dev(y, p, c, m))
        cp.start()
        back.append(cp)
    ret_between[z] = ret[:, :, z]
    for p in reversed(z_peers):
        copy(ret.at[:, :, p], ret_between.at[p], r_send.at[p], r_recv.at[p],
             dev(y, p, c, m)).wait_recv()
    for yy, co in plane:
        cp = copy(ret_between.at[:, yy, co], ret_got.at[y, c], t_send.at[yy * NC + co],
                  t_recv.at[y * NC + c], dev(yy, z, co, m))
        cp.start()
        back.append(cp)
    ret_got[y, c] = ret_between[:, y, c]
    spot = lax.broadcasted_iota(jnp.int32, (N_DP, count), 0)
    spot_z, spot_yc = lax.rem(spot, NZ), lax.div(spot, NZ)
    spot = (lax.div(spot_yc, NC) * NZ + spot_z) * NC + lax.rem(spot_yc, NC)
    hit = jnp.where(spot.astype(f32) == owner, 1.0, 0.0)
    for yy, co in plane:
        copy(ret_between.at[:, yy, co], ret_got.at[yy, co], t_send.at[yy * NC + co],
             t_recv.at[yy * NC + co], dev(yy, z, co, m)).wait_recv()
    for cp in back:
        cp.wait_send()
    table = lax.dot_general(ret_got[:, :, :, 0, :].reshape(N_DP, BLK), hit,
                            (((0,), (0,)), ((), ())), precision=HIGH, preferred_element_type=f32)
    score = jnp.zeros((1, count), f32)
    for k in range(PAIR):
        score = jnp.where(rank == float(k), table[k:k + 1, :], score)
    out_ref[...] = score


def local(embeddings, cluster_ids):
    row_count, feat_width = embeddings.shape
    dp_count = lax.axis_size("dp")
    f32, bf16 = jnp.float32, jnp.bfloat16
    dma = pltpu.SemaphoreType.DMA
    scratch = [
        pltpu.VMEM((NC, NY, NZ, NB, BLK), f32),
        pltpu.VMEM((NY, NZ, NB, BLK), f32),
        pltpu.VMEM((NY, NZ, NB, BLK), f32),
        pltpu.VMEM((NY, NZ, NB, BLK), f32),
        pltpu.VMEM((NZ, NB, BLK), f32),
        pltpu.VMEM((NZ, NB, BLK), f32),
        pltpu.VMEM((NX, NC, NY, NZ, NB, BLK), f32),
        pltpu.VMEM((NX * N_DP * 8, BLK), f32),
        pltpu.VMEM((N_DP * (NB + 2), BLK), f32),
        pltpu.VMEM((NY, NZ, NC, NB + 2, BLK), bf16),
        pltpu.VMEM((NY, NC, NZ, NB + 2, BLK), bf16),
        pltpu.VMEM((NX, NY, NC, NZ, NB + 2, BLK), bf16),
        pltpu.VMEM((D, D), f32),
        pltpu.VMEM((D, 6 * BLK), bf16),
        pltpu.VMEM((6 * BLK, D), bf16),
        pltpu.VMEM((D, D), bf16),
        pltpu.VMEM((PAIR * N_DP, D), bf16),
        pltpu.VMEM((NY, NC, NZ, 1, BLK), f32),
        pltpu.VMEM((NZ, NY, NC, 1, BLK), f32),
        pltpu.VMEM((NY, NC, NZ, 1, BLK), f32),
        dma, dma, dma((NY,)), dma((NY,)), dma((NZ,)), dma((NZ,)),
        dma((NZ,)), dma((NZ,)), dma((NY,)), dma((NY,)), dma((NX,)), dma((NX,)),
        dma((NX,)), dma((NX,)), dma((NY,)), dma((NY,)), dma((13,)), dma((13,)),
        dma((NY * NC,)), dma((NY * NC,)), dma((NZ,)), dma((NZ,)), dma((NX,)), dma((NX,)), dma((2,)), dma((2,)),
        dma((NZ,)), dma((NZ,)), dma((NY * NC,)), dma((NY * NC,)),
    ]
    vm = pl.BlockSpec(memory_space=pltpu.VMEM)
    scores = pl.pallas_call(
        functools.partial(kernel, float(row_count * dp_count)),
        out_shape=jax.ShapeDtypeStruct((1, row_count), f32),
        in_specs=[vm, vm],
        out_specs=vm,
        scratch_shapes=scratch,
        name="dedup",
        compiler_params=pltpu.CompilerParams(collective_id=0, has_side_effects=True),
    )(embeddings, cluster_ids.reshape(1, row_count))
    return scores.reshape(row_count)


def solution(mesh):
    in_specs = (P("dp", None), P("dp"))
    out_specs = P("dp")
    return jax.shard_map(local, mesh=mesh, in_specs=in_specs, out_specs=out_specs, check_vma=False)
```

```python
import functools

import jax
import jax.numpy as jnp
from jax import lax
from jax.experimental import pallas as pl
from jax.experimental.pallas import tpu as pltpu
from jax.sharding import PartitionSpec as P

CPO = 4
NX, NC, NY, NZ = 4, 2, 4, 16
BLK = 128
NB = 6
D = NB * BLK
N_DP = NC * NY * NZ
PAIR = 4
GATHER_AT = 1
RELAY_AT = 3
MESH = pl.DeviceIdType.MESH
HIGH = lax.Precision.HIGHEST


def split3(value):
    high = value.astype(jnp.bfloat16)
    rest = value - high.astype(jnp.float32)
    mid = rest.astype(jnp.bfloat16)
    low = (rest - mid.astype(jnp.float32)).astype(jnp.bfloat16)
    return high, mid, low


def lower_inverse(block):
    lane = lax.broadcasted_iota(jnp.int32, (8, BLK), 1)
    sub = lax.broadcasted_iota(jnp.int32, (8, BLK), 0)
    groups = BLK // 8
    wide = (8, BLK)
    picks = [jnp.full(wide, q, jnp.int32) for q in range(8)]
    scales = []
    for t in range(groups):
        own = block[t]
        base = 8 * t
        cols = [jnp.broadcast_to(own[:, base + q:base + q + 1], wide) for q in range(8)]
        piv = [[None] * 8 for _ in range(8)]
        for q in range(8):
            for r in range(q, 8):
                piv[q][r] = jnp.take_along_axis(cols[r], picks[q], axis=0)
        mult = [[None] * 8 for _ in range(8)]
        inv = [None] * 8
        scale = None
        for q in range(0, 8, 2):
            cross, last = piv[q][q + 1], piv[q + 1][q + 1]
            minor = piv[q][q] * last - cross * cross
            inv[q] = 1.0 / piv[q][q]
            inv[q + 1] = piv[q][q] * (1.0 / minor)
            mult[q][q + 1] = cross * inv[q]
            piv[q + 1][q + 1] = minor * inv[q]
            for r in range(q + 2, 8):
                mult[q][r] = piv[q][r] * inv[q]
                piv[q + 1][r] = piv[q + 1][r] - mult[q][q + 1] * piv[q][r]
                mult[q + 1][r] = piv[q + 1][r] * inv[q + 1]
            for r in range(q + 2, 8):
                for s in range(r, 8):
                    piv[r][s] = (piv[r][s] - mult[q][r] * piv[q][s]) - mult[q + 1][r] * piv[q + 1][s]
        for q in range(8):
            scale = piv[q][q] if scale is None else jnp.where(sub == q, piv[q][q], scale)
        root = lax.rsqrt(scale)
        scale = root * (1.5 - 0.5 * scale * root * root)
        scales.append(scale)
        rows = []
        for q in range(8):
            row = jnp.broadcast_to(own[q:q + 1, :], wide)
            row = jnp.where(lane == base + q, inv[q], row * inv[q])
            rows.append(row)
            masked = jnp.where(sub > q, cols[q], 0.0)
            own = jnp.where((lane == base + q) & (sub > q), 0.0, own) - masked * row
            for r in range(q + 1, 8):
                cols[r] = cols[r] - masked * mult[q][r]
        block[t] = own
        if t + 1 == groups:
            continue
        cur = block[t + 1]
        coef = [jnp.broadcast_to(cur[:, base + q:base + q + 1], wide) for q in range(8)]
        for q in range(8):
            cur = jnp.where(lane == base + q, 0.0, cur) - coef[q] * rows[q]
            for r in range(q + 1, 8):
                coef[r] = coef[r] - coef[q] * mult[q][r]
        block[t + 1] = cur
        if t + 2 == groups:
            continue
        panel = (lane >= base) & (lane < base + 8)
        rows = [jnp.where((lane > base + q) & (lane < base + 8), 0.0, rows[q]) for q in range(8)]
        right = rows[0]
        for q in range(1, 8):
            right = jnp.where(sub == q, rows[q], right)
        ah, am, al = split3(own)
        bh, bm, bl = split3(right)
        upd = lax.dot_general(jnp.concatenate([ah, ah, am, ah, al, am], axis=0),
                              jnp.concatenate([bh, bm, bh, bl, bh, bm], axis=0),
                              (((0,), (0,)), ((), ())), preferred_element_type=jnp.float32)
        for s in range(t + 2, groups):
            block[s] = jnp.where(panel, 0.0, block[s]) - upd[8 * s:8 * s + 8, :]
    for t in range(groups):
        diff = lane - sub - 8 * t
        block[t] = scales[t] * jnp.where(diff < 0, block[t], jnp.where(diff == 0, 1.0, 0.0))
    return block


def stack_left(value, axis):
    high, mid, low = split3(value)
    return jnp.concatenate([high, high, mid, high, low, mid], axis=axis)


def stack_right(value, axis):
    high, mid, low = split3(value)
    return jnp.concatenate([high, mid, high, low, high, mid], axis=axis)


def mm(a, b):
    return lax.dot_general(a, b, (((1,), (0,)), ((), ())), preferred_element_type=jnp.float32)


def kernel(row_total, x_ref, ids_ref, out_ref,
           part, got_c, half, got_y, quarter, got_z, mom, flat,
           stage, send_rows, between, got, work, left, right, white, rows,
           ret, ret_between, ret_got,
           c_send, c_recv, y_send, y_recv, z_send, z_recv,
           gz_send, gz_recv, a_send, a_recv, b_send, b_recv,
           a2_send, a2_recv, b2_send, b2_recv, gc_send, gc_recv,
           d_send, d_recv, e_send, e_recv, x_send, x_recv, f_send, f_recv,
           r_send, r_recv, t_send, t_recv):
    f32, bf16 = jnp.float32, jnp.bfloat16
    m = lax.axis_index("mp")
    d = lax.axis_index("dp")
    c = lax.rem(d, 2)
    z = lax.rem(lax.div(d, 2), NZ)
    y = lax.div(d, 2 * NZ)

    def dev(yy, zz, cc, mm):
        return ((yy * NZ + zz) * 2 + cc, mm)

    sibling = dev(y, z, 1 - c, m)
    y_peers = [lax.rem(y + o, NY) for o in (2, 1, 3)]
    z_peers = [lax.rem(z + o, NZ) for o in (8, 7, 9, 6, 10, 5, 11, 4, 12, 3, 13, 2, 14, 1, 15)]
    x_peers = [lax.rem(m + o, NX) for o in (2, 1, 3)]
    plane = [(lax.rem(y + o, NY), co) for o in (2, 1, 3) for co in (1 - c, c)] + [(y, 1 - c)]
    barrier = pltpu.get_barrier_semaphore()
    everyone = ([dev(y, p, c, m) for p in z_peers] + [dev(yy, z, co, m) for yy, co in plane]
                + [dev(y, z, c, p) for p in x_peers])
    for peer in everyone:
        pl.semaphore_signal(barrier, inc=1, device_id=peer, device_id_type=MESH)

    for i in range(NB):
        j = lax.rem(i + m, NB)
        lhs = x_ref[:, i * BLK:(i + 1) * BLK]
        rhs = x_ref[:, pl.ds(pl.multiple_of(j * BLK, BLK), BLK)]
        prod = lax.dot_general(lhs, rhs, (((0,), (0,)), ((), ())),
                               preferred_element_type=f32)
        part[:, :, :, i, :] = prod.reshape(NC, NY, NZ, BLK)

    count = x_ref.shape[0]
    owner = lax.div(ids_ref[...], CPO)
    within = (ids_ref[...] - owner * CPO + 1).astype(f32)
    owner = owner.astype(f32)
    owner_row = jnp.broadcast_to(owner, (count, count))
    first = lax.broadcasted_iota(jnp.int32, (count, count), 0)
    second = lax.broadcasted_iota(jnp.int32, (count, count), 1)
    earlier = (owner_row == owner_row.T) & (first < second)
    rank = jnp.sum(jnp.where(earlier, 1.0, 0.0), axis=0, keepdims=True)
    owner_iota = lax.broadcasted_iota(jnp.int32, (N_DP, count), 0).astype(f32)
    pick = jnp.where((owner_iota == owner) & (rank == m.astype(f32)), 1.0, 0.0)
    picked = lax.dot_general(pick.astype(bf16), x_ref[...], (((1,), (0,)), ((), ())),
                             preferred_element_type=f32)
    label = jnp.sum(pick * within, axis=1, keepdims=True) - 1.0
    for i in range(NB):
        stage[pl.ds(i, N_DP, stride=NB + 2), :] = picked[:, i * BLK:(i + 1) * BLK]
    stage[pl.ds(NB, N_DP, stride=NB + 2), :] = jnp.broadcast_to(label, (N_DP, BLK))
    stage[pl.ds(NB + 1, N_DP, stride=NB + 2), :] = jnp.zeros((N_DP, BLK), f32)
    send_rows[...] = stage[...].reshape(NY, NZ, NC, NB + 2, BLK).astype(bf16)
    between[y, c] = send_rows[y, :, c]
    pl.semaphore_wait(barrier, len(everyone))

    def copy(src, dst, send, recv, device):
        return pltpu.make_async_remote_copy(
            src_ref=src, dst_ref=dst, send_sem=send, recv_sem=recv,
            device_id=device, device_id_type=MESH)

    sent = []
    order = y_peers + [y]
    for p in order:
        cp = copy(part.at[1 - c, p], got_c.at[p], c_send.at[p], c_recv.at[p], sibling)
        cp.start()
        sent.append(cp)
    for p in order:
        copy(part.at[1 - c, p], got_c.at[p], c_send.at[p], c_recv.at[p], sibling).wait_recv()
        half[p] = part[c, p] + got_c[p]
        if p is not y:
            cp = copy(half.at[p], got_y.at[y], y_send.at[p], y_recv.at[y], dev(p, z, c, m))
            cp.start()
            sent.append(cp)
    total = half[y]
    for p in y_peers:
        copy(half.at[p], got_y.at[p], y_send.at[p], y_recv.at[p], dev(p, z, c, m)).wait_recv()
        total = total + got_y[p]
    quarter[...] = total
    for p in z_peers:
        cp = copy(quarter.at[p], got_z.at[z], z_send.at[p], z_recv.at[z], dev(y, p, c, m))
        cp.start()
        sent.append(cp)
    for yy, co in plane:
        cp = copy(send_rows.at[yy, :, co], between.at[y, c], d_send.at[yy * NC + co],
                  d_recv.at[y * NC + c], dev(yy, z, co, m))
        cp.start()
        sent.append(cp)
    row = quarter[z]
    for p in reversed(z_peers):
        copy(quarter.at[p], got_z.at[p], z_send.at[p], z_recv.at[p], dev(y, p, c, m)).wait_recv()
        row = row + got_z[p]
    mom[m, c, y, z] = row
    for p in z_peers:
        cp = copy(mom.at[m, c, y, z], mom.at[m, c, y, z], gz_send.at[p], gz_recv.at[z],
                  dev(y, p, c, m))
        cp.start()
        sent.append(cp)

    for p in reversed(z_peers):
        copy(mom.at[m, c, y, p], mom.at[m, c, y, p], gz_send.at[p], gz_recv.at[p],
             dev(y, p, c, m)).wait_recv()
    for yy, co in plane:
        copy(send_rows.at[yy, :, co], between.at[yy, co], d_send.at[yy * NC + co],
             d_recv.at[yy * NC + co], dev(yy, z, co, m)).wait_recv()
    late = []
    for p in z_peers:
        cp = copy(between.at[:, :, p], got.at[m, :, :, z], e_send.at[p], e_recv.at[z],
                  dev(y, p, c, m))
        cp.start()
        late.append(cp)
    got[m, :, :, z] = between[:, :, z]
    lo, hi = pl.ds(0, NZ // 2), pl.ds(NZ // 2, NZ // 2)

    def piece(n, core):
        kind, peer = divmod(n + 2, 3)
        return (mom.at[m, core, y],
                mom.at[m, core, y_peers[peer], lo],
                mom.at[x_peers[peer], core, y, hi],
                mom.at[x_peers[peer], core, :, lo],
                mom.at[:, core, y_peers[peer], hi])[kind]

    def pass_on(n):
        cp = copy(piece(n, c), piece(n, c), gc_send.at[n], gc_recv.at[n], sibling)
        cp.start()
        sent.append(cp)

    for p in y_peers:
        cp = copy(mom.at[m, c, y, lo], mom.at[m, c, y, lo], a_send.at[p], a_recv.at[y],
                  dev(p, z, c, m))
        cp.start()
        sent.append(cp)
    for p in x_peers:
        cp = copy(mom.at[m, c, y, hi], mom.at[m, c, y, hi], b_send.at[p], b_recv.at[m],
                  dev(y, z, c, p))
        cp.start()
        sent.append(cp)

    def low_piece(q):
        for p in x_peers:
            cp = copy(mom.at[m, c, q, lo], mom.at[m, c, q, lo], a2_send.at[p * NY + q],
                      a2_recv.at[m * NY + q], dev(y, z, c, p))
            cp.start()
            sent.append(cp)

    def high_piece(q):
        for p in y_peers:
            cp = copy(mom.at[q, c, y, hi], mom.at[q, c, y, hi], b2_send.at[p * NX + q],
                      b2_recv.at[y * NX + q], dev(p, z, c, m))
            cp.start()
            sent.append(cp)

    low_piece(y)
    high_piece(m)
    pass_on(0)
    for n in (1, 2, 0):
        p = y_peers[n]
        copy(mom.at[m, c, p, lo], mom.at[m, c, p, lo], a_send.at[p], a_recv.at[p],
             dev(p, z, c, m)).wait_recv()
        low_piece(p)
        pass_on(1 + n)
        p = x_peers[n]
        copy(mom.at[p, c, y, hi], mom.at[p, c, y, hi], b_send.at[p], b_recv.at[p],
             dev(y, z, c, p)).wait_recv()
        high_piece(p)
        pass_on(4 + n)
    for n in (1, 2, 0):
        p = x_peers[n]
        for q in range(NY):
            copy(mom.at[p, c, q, lo], mom.at[p, c, q, lo], a2_send.at[p * NY + q],
                 a2_recv.at[p * NY + q], dev(y, z, c, p)).wait_recv()
        pass_on(7 + n)
        p = y_peers[n]
        for q in range(NX):
            copy(mom.at[q, c, p, hi], mom.at[q, c, p, hi], b2_send.at[p * NX + q],
                 b2_recv.at[p * NX + q], dev(p, z, c, m)).wait_recv()
        pass_on(10 + n)
    for n in range(13):
        copy(piece(n, 1 - c), piece(n, 1 - c), gc_send.at[n], gc_recv.at[n], sibling).wait_recv()
    for cp in sent:
        cp.wait_send()

    for i in range(0, NB, 2):
        white[i * BLK:(i + 1) * BLK, (i + 1) * BLK:(i + 2) * BLK] = jnp.zeros((BLK, BLK), bf16)
    scale = 1.0 / row_total
    eye = jnp.where(lax.broadcasted_iota(jnp.int32, (BLK, BLK), 0)
                    == lax.broadcasted_iota(jnp.int32, (BLK, BLK), 1), 0.001, 0.0)

    def at(i, j):
        return (slice(i * BLK, (i + 1) * BLK), slice(j * BLK, (j + 1) * BLK))

    def moment_block(g, i):
        return flat[pl.ds(g * N_DP * 8 + i, N_DP, stride=8), :] * scale

    @pl.loop(0, NX * N_DP // 16)
    def _(b):
        for r in range(16):
            flat[pl.ds(pl.multiple_of(b * BLK, BLK) + 8 * r, NB), :] = (
                mom[lax.div(b, 8), lax.div(lax.rem(b, 8), 4), lax.rem(b, 4), r])

    for i in range(NB):
        for g in range(4):
            j = i + g
            if j < NB:
                val = moment_block(g, i)
                work[at(i, j)] = val + eye if g == 0 else val
            elif g < 3:
                work[at(j - NB, i)] = moment_block(g, i).T

    labels = []
    following, previous, opposite = (lax.rem(m + o, NX) for o in (1, 3, 2))
    halves = (pl.ds(0, NY // 2), pl.ds(NY // 2, NY // 2))
    corner = work[at(0, 0)]
    for kk in range(NB):
        if kk == GATHER_AT:
            for p in z_peers:
                copy(between.at[:, :, p], got.at[m, :, :, p], e_send.at[p], e_recv.at[p],
                     dev(y, p, c, m)).wait_recv()
            for p in (following, previous):
                cp = copy(got.at[m], got.at[m], x_send.at[p], x_recv.at[m], (d, p))
                cp.start()
                late.append(cp)
        if kk == RELAY_AT:
            for p in (following, previous):
                copy(got.at[p], got.at[p], x_send.at[p], x_recv.at[p], (d, p)).wait_recv()
            for n, (source, p) in enumerate(((previous, following), (following, previous))):
                part_of = got.at[source, halves[n]]
                cp = copy(part_of, part_of, f_send.at[n], f_recv.at[n], (d, p))
                cp.start()
                late.append(cp)
        if kk == NB - 1:
            for n, p in enumerate((previous, following)):
                part_of = got.at[opposite, halves[n]]
                copy(part_of, part_of, f_send.at[n], f_recv.at[n], (d, p)).wait_recv()
            for k in range(PAIR):
                stage[...] = got[k].astype(f32).reshape(N_DP * (NB + 2), BLK)
                for i in range(NB):
                    rows[k * N_DP:(k + 1) * N_DP, i * BLK:(i + 1) * BLK] = (
                        stage[pl.ds(i, N_DP, stride=NB + 2), :].astype(bf16))
                labels.append(stage[pl.ds(NB, N_DP, stride=NB + 2), :])
        inverse = jnp.concatenate(
            lower_inverse([corner[8 * t:8 * t + 8, :] for t in range(BLK // 8)]), axis=0)
        rk = slice(kk * BLK, (kk + 1) * BLK)
        line = mm(stack_left(inverse, 1), stack_right(work[rk, :], 0))
        white[at(kk, kk)] = inverse.astype(bf16)
        if kk:
            white[rk, :kk * BLK] = line[:, :kk * BLK].astype(bf16)
        if kk == NB - 1:
            break
        done = (kk + 1) * BLK
        left[done:, :] = stack_left(line[:, done:].T, 1)
        right[:, done:] = stack_right(line[:, done:], 0)
        nxt = at(kk + 1, kk + 1)
        corner = work[nxt] - mm(left[nxt[0], :], right[:, nxt[1]])
        right[:, :done] = stack_right(
            jnp.concatenate([line[:, :kk * BLK], inverse], axis=1) if kk else inverse, 0)
        old = mm(left[done:, :], right[:, :done])
        if kk:
            work[done:, :kk * BLK] = work[done:, :kk * BLK] - old[:, :kk * BLK]
        work[done:, rk] = -old[:, rk]
        for i in range(kk + 1, NB, 2):
            ri = slice(i * BLK, min(i + 2, NB) * BLK)
            work[ri, i * BLK:] = work[ri, i * BLK:] - mm(left[ri, :], right[:, i * BLK:])

    for cp in late:
        cp.wait_send()
    wide = 2 * BLK
    whitened = jnp.concatenate(
        [lax.dot_general(rows[:, :n + wide], white[n:n + wide, :n + wide],
                         (((1,), (1,)), ((), ())), preferred_element_type=f32)
         for n in range(0, D, wide)], axis=1).astype(bf16)
    widened = whitened.astype(f32)
    square_sum = jnp.sum(widened * widened, axis=1, keepdims=True)
    rows[...] = (widened * lax.rsqrt(square_sum + 1e-06)).astype(bf16)
    lane = lax.broadcasted_iota(jnp.int32, (N_DP, N_DP), 1)
    other = lax.broadcasted_iota(jnp.int32, (N_DP, N_DP), 0) != lane
    flipped = [value.T for value in labels]
    reply = jnp.zeros((N_DP, N_DP), f32)
    for a in range(PAIR):
        sim = lax.dot_general(rows[a * N_DP:(a + 1) * N_DP, :], rows[...],
                              (((1,), (1,)), ((), ())), preferred_element_type=f32)
        best = jnp.full((N_DP, N_DP), -1.0, f32)
        for b in range(PAIR):
            same = (labels[a] == flipped[b]) & (labels[a] >= 0.0)
            if a == b:
                same = same & other
            best = jnp.maximum(best, jnp.where(same, sim[:, b * N_DP:(b + 1) * N_DP], -1.0))
        reply = jnp.where(lane == a, jnp.max(best, axis=1, keepdims=True), reply)
    ret[:, :, :, 0, :] = reply.reshape(NY, NC, NZ, BLK)
    back = []
    for p in z_peers:
        cp = copy(ret.at[:, :, p], ret_between.at[z], r_send.at[p], r_recv.at[z], dev(y, p, c, m))
        cp.start()
        back.append(cp)
    ret_between[z] = ret[:, :, z]
    for p in reversed(z_peers):
        copy(ret.at[:, :, p], ret_between.at[p], r_send.at[p], r_recv.at[p],
             dev(y, p, c, m)).wait_recv()
    for yy, co in plane:
        cp = copy(ret_between.at[:, yy, co], ret_got.at[y, c], t_send.at[yy * NC + co],
                  t_recv.at[y * NC + c], dev(yy, z, co, m))
        cp.start()
        back.append(cp)
    ret_got[y, c] = ret_between[:, y, c]
    spot = lax.broadcasted_iota(jnp.int32, (N_DP, count), 0)
    spot_z, spot_yc = lax.rem(spot, NZ), lax.div(spot, NZ)
    spot = (lax.div(spot_yc, NC) * NZ + spot_z) * NC + lax.rem(spot_yc, NC)
    hit = jnp.where(spot.astype(f32) == owner, 1.0, 0.0)
    for yy, co in plane:
        copy(ret_between.at[:, yy, co], ret_got.at[yy, co], t_send.at[yy * NC + co],
             t_recv.at[yy * NC + co], dev(yy, z, co, m)).wait_recv()
    for cp in back:
        cp.wait_send()
    table = lax.dot_general(ret_got[:, :, :, 0, :].reshape(N_DP, BLK), hit,
                            (((0,), (0,)), ((), ())), precision=HIGH, preferred_element_type=f32)
    score = jnp.zeros((1, count), f32)
    for k in range(PAIR):
        score = jnp.where(rank == float(k), table[k:k + 1, :], score)
    out_ref[...] = score


def local(embeddings, cluster_ids):
    row_count, feat_width = embeddings.shape
    dp_count = lax.axis_size("dp")
    f32, bf16 = jnp.float32, jnp.bfloat16
    dma = pltpu.SemaphoreType.DMA
    scratch = [
        pltpu.VMEM((NC, NY, NZ, NB, BLK), f32),
        pltpu.VMEM((NY, NZ, NB, BLK), f32),
        pltpu.VMEM((NY, NZ, NB, BLK), f32),
        pltpu.VMEM((NY, NZ, NB, BLK), f32),
        pltpu.VMEM((NZ, NB, BLK), f32),
        pltpu.VMEM((NZ, NB, BLK), f32),
        pltpu.VMEM((NX, NC, NY, NZ, NB, BLK), f32),
        pltpu.VMEM((NX * N_DP * 8, BLK), f32),
        pltpu.VMEM((N_DP * (NB + 2), BLK), f32),
        pltpu.VMEM((NY, NZ, NC, NB + 2, BLK), bf16),
        pltpu.VMEM((NY, NC, NZ, NB + 2, BLK), bf16),
        pltpu.VMEM((NX, NY, NC, NZ, NB + 2, BLK), bf16),
        pltpu.VMEM((D, D), f32),
        pltpu.VMEM((D, 6 * BLK), bf16),
        pltpu.VMEM((6 * BLK, D), bf16),
        pltpu.VMEM((D, D), bf16),
        pltpu.VMEM((PAIR * N_DP, D), bf16),
        pltpu.VMEM((NY, NC, NZ, 1, BLK), f32),
        pltpu.VMEM((NZ, NY, NC, 1, BLK), f32),
        pltpu.VMEM((NY, NC, NZ, 1, BLK), f32),
        dma((NY,)), dma((NY,)), dma((NY,)), dma((NY,)), dma((NZ,)), dma((NZ,)),
        dma((NZ,)), dma((NZ,)), dma((NY,)), dma((NY,)), dma((NX,)), dma((NX,)),
        dma((NX * NY,)), dma((NX * NY,)), dma((NX * NY,)), dma((NX * NY,)),
        dma((13,)), dma((13,)),
        dma((NY * NC,)), dma((NY * NC,)), dma((NZ,)), dma((NZ,)), dma((NX,)), dma((NX,)), dma((2,)), dma((2,)),
        dma((NZ,)), dma((NZ,)), dma((NY * NC,)), dma((NY * NC,)),
    ]
    vm = pl.BlockSpec(memory_space=pltpu.VMEM)
    scores = pl.pallas_call(
        functools.partial(kernel, float(row_count * dp_count)),
        out_shape=jax.ShapeDtypeStruct((1, row_count), f32),
        in_specs=[vm, vm],
        out_specs=vm,
        scratch_shapes=scratch,
        name="dedup",
        compiler_params=pltpu.CompilerParams(collective_id=0, has_side_effects=True),
    )(embeddings, cluster_ids.reshape(1, row_count))
    return scores.reshape(row_count)


def solution(mesh):
    in_specs = (P("dp", None), P("dp"))
    out_specs = P("dp")
    return jax.shard_map(local, mesh=mesh, in_specs=in_specs, out_specs=out_specs, check_vma=False)
```

```python
import functools

import jax
import jax.numpy as jnp
from jax import lax
from jax.experimental import pallas as pl
from jax.experimental.pallas import tpu as pltpu
from jax.sharding import PartitionSpec as P

CPO = 4
NX, NC, NY, NZ = 4, 2, 4, 16
BLK = 128
NB = 6
D = NB * BLK
N_DP = NC * NY * NZ
PAIR = 4
GATHER_AT = 1
RELAY_AT = 3
MESH = pl.DeviceIdType.MESH
HIGH = lax.Precision.HIGHEST


def split3(value):
    high = value.astype(jnp.bfloat16)
    rest = value - high.astype(jnp.float32)
    mid = rest.astype(jnp.bfloat16)
    low = (rest - mid.astype(jnp.float32)).astype(jnp.bfloat16)
    return high, mid, low


def lower_inverse(block):
    lane = lax.broadcasted_iota(jnp.int32, (8, BLK), 1)
    sub = lax.broadcasted_iota(jnp.int32, (8, BLK), 0)
    groups = BLK // 8
    wide = (8, BLK)
    picks = [jnp.full(wide, q, jnp.int32) for q in range(8)]
    scales = []
    for t in range(groups):
        own = block[t]
        base = 8 * t
        cols = [jnp.broadcast_to(own[:, base + q:base + q + 1], wide) for q in range(8)]
        piv = [[None] * 8 for _ in range(8)]
        for q in range(8):
            for r in range(q, 8):
                piv[q][r] = jnp.take_along_axis(cols[r], picks[q], axis=0)
        mult = [[None] * 8 for _ in range(8)]
        inv = [None] * 8
        scale = None
        for q in range(0, 8, 2):
            cross, last = piv[q][q + 1], piv[q + 1][q + 1]
            minor = piv[q][q] * last - cross * cross
            inv[q] = 1.0 / piv[q][q]
            inv[q + 1] = piv[q][q] * (1.0 / minor)
            mult[q][q + 1] = cross * inv[q]
            piv[q + 1][q + 1] = minor * inv[q]
            for r in range(q + 2, 8):
                mult[q][r] = piv[q][r] * inv[q]
                piv[q + 1][r] = piv[q + 1][r] - mult[q][q + 1] * piv[q][r]
                mult[q + 1][r] = piv[q + 1][r] * inv[q + 1]
            for r in range(q + 2, 8):
                for s in range(r, 8):
                    piv[r][s] = (piv[r][s] - mult[q][r] * piv[q][s]) - mult[q + 1][r] * piv[q + 1][s]
        for q in range(8):
            scale = piv[q][q] if scale is None else jnp.where(sub == q, piv[q][q], scale)
        root = lax.rsqrt(scale)
        scale = root * (1.5 - 0.5 * scale * root * root)
        scales.append(scale)
        rows = []
        for q in range(8):
            row = jnp.broadcast_to(own[q:q + 1, :], wide)
            row = jnp.where(lane == base + q, inv[q], row * inv[q])
            rows.append(row)
            masked = jnp.where(sub > q, cols[q], 0.0)
            own = jnp.where((lane == base + q) & (sub > q), 0.0, own) - masked * row
            for r in range(q + 1, 8):
                cols[r] = cols[r] - masked * mult[q][r]
        block[t] = own
        if t + 1 == groups:
            continue
        cur = block[t + 1]
        coef = [jnp.broadcast_to(cur[:, base + q:base + q + 1], wide) for q in range(8)]
        for q in range(8):
            cur = jnp.where(lane == base + q, 0.0, cur) - coef[q] * rows[q]
            for r in range(q + 1, 8):
                coef[r] = coef[r] - coef[q] * mult[q][r]
        block[t + 1] = cur
        if t + 2 == groups:
            continue
        panel = (lane >= base) & (lane < base + 8)
        rows = [jnp.where((lane > base + q) & (lane < base + 8), 0.0, rows[q]) for q in range(8)]
        right = rows[0]
        for q in range(1, 8):
            right = jnp.where(sub == q, rows[q], right)
        ah, am, al = split3(own)
        bh, bm, bl = split3(right)
        upd = lax.dot_general(jnp.concatenate([ah, ah, am, ah, al, am], axis=0),
                              jnp.concatenate([bh, bm, bh, bl, bh, bm], axis=0),
                              (((0,), (0,)), ((), ())), preferred_element_type=jnp.float32)
        for s in range(t + 2, groups):
            block[s] = jnp.where(panel, 0.0, block[s]) - upd[8 * s:8 * s + 8, :]
    for t in range(groups):
        diff = lane - sub - 8 * t
        block[t] = scales[t] * jnp.where(diff < 0, block[t], jnp.where(diff == 0, 1.0, 0.0))
    return block


def stack_left(value, axis):
    high, mid, low = split3(value)
    return jnp.concatenate([high, high, mid, high, low, mid], axis=axis)


def stack_right(value, axis):
    high, mid, low = split3(value)
    return jnp.concatenate([high, mid, high, low, high, mid], axis=axis)


def mm(a, b):
    return lax.dot_general(a, b, (((1,), (0,)), ((), ())), preferred_element_type=jnp.float32)


def kernel(row_total, x_ref, ids_ref, out_ref,
           part, got_c, half, got_y, quarter, got_z, mom, flat,
           stage, send_rows, between, got, work, left, right, white, rows,
           ret, ret_between, ret_got,
           c_send, c_recv, y_send, y_recv, z_send, z_recv,
           gz_send, gz_recv, a_send, a_recv, b_send, b_recv,
           a2_send, a2_recv, b2_send, b2_recv, gc_send, gc_recv,
           d_send, d_recv, e_send, e_recv, x_send, x_recv, f_send, f_recv,
           r_send, r_recv, t_send, t_recv):
    f32, bf16 = jnp.float32, jnp.bfloat16
    m = lax.axis_index("mp")
    d = lax.axis_index("dp")
    c = lax.rem(d, 2)
    z = lax.rem(lax.div(d, 2), NZ)
    y = lax.div(d, 2 * NZ)

    def dev(yy, zz, cc, mm):
        return ((yy * NZ + zz) * 2 + cc, mm)

    sibling = dev(y, z, 1 - c, m)
    y_peers = [lax.rem(y + o, NY) for o in (2, 1, 3)]
    z_peers = [lax.rem(z + o, NZ) for o in (8, 7, 9, 6, 10, 5, 11, 4, 12, 3, 13, 2, 14, 1, 15)]
    x_peers = [lax.rem(m + o, NX) for o in (2, 1, 3)]
    plane = [(lax.rem(y + o, NY), co) for o in (2, 1, 3) for co in (1 - c, c)] + [(y, 1 - c)]
    barrier = pltpu.get_barrier_semaphore()
    everyone = ([dev(y, p, c, m) for p in z_peers] + [dev(yy, z, co, m) for yy, co in plane]
                + [dev(y, z, c, p) for p in x_peers])
    for peer in everyone:
        pl.semaphore_signal(barrier, inc=1, device_id=peer, device_id_type=MESH)

    for i in range(NB):
        j = lax.rem(i + m, NB)
        lhs = x_ref[:, i * BLK:(i + 1) * BLK]
        rhs = x_ref[:, pl.ds(pl.multiple_of(j * BLK, BLK), BLK)]
        prod = lax.dot_general(lhs, rhs, (((0,), (0,)), ((), ())),
                               preferred_element_type=f32)
        part[:, :, :, i, :] = prod.reshape(NC, NY, NZ, BLK)

    count = x_ref.shape[0]
    owner = lax.div(ids_ref[...], CPO)
    within = (ids_ref[...] - owner * CPO + 1).astype(f32)
    owner = owner.astype(f32)
    owner_row = jnp.broadcast_to(owner, (count, count))
    first = lax.broadcasted_iota(jnp.int32, (count, count), 0)
    second = lax.broadcasted_iota(jnp.int32, (count, count), 1)
    earlier = (owner_row == owner_row.T) & (first < second)
    rank = jnp.sum(jnp.where(earlier, 1.0, 0.0), axis=0, keepdims=True)
    owner_iota = lax.broadcasted_iota(jnp.int32, (N_DP, count), 0).astype(f32)
    pick = jnp.where((owner_iota == owner) & (rank == m.astype(f32)), 1.0, 0.0)
    picked = lax.dot_general(pick.astype(bf16), x_ref[...], (((1,), (0,)), ((), ())),
                             preferred_element_type=f32)
    label = jnp.sum(pick * within, axis=1, keepdims=True) - 1.0
    for i in range(NB):
        stage[pl.ds(i, N_DP, stride=NB + 2), :] = picked[:, i * BLK:(i + 1) * BLK]
    stage[pl.ds(NB, N_DP, stride=NB + 2), :] = jnp.broadcast_to(label, (N_DP, BLK))
    stage[pl.ds(NB + 1, N_DP, stride=NB + 2), :] = jnp.zeros((N_DP, BLK), f32)
    send_rows[...] = stage[...].reshape(NY, NZ, NC, NB + 2, BLK).astype(bf16)
    between[y, c] = send_rows[y, :, c]
    pl.semaphore_wait(barrier, len(everyone))

    def copy(src, dst, send, recv, device):
        return pltpu.make_async_remote_copy(
            src_ref=src, dst_ref=dst, send_sem=send, recv_sem=recv,
            device_id=device, device_id_type=MESH)

    sent = []
    order = y_peers + [y]
    for p in order:
        cp = copy(part.at[1 - c, p], got_c.at[p], c_send.at[p], c_recv.at[p], sibling)
        cp.start()
        sent.append(cp)
    for p in order:
        copy(part.at[1 - c, p], got_c.at[p], c_send.at[p], c_recv.at[p], sibling).wait_recv()
        half[p] = part[c, p] + got_c[p]
        if p is not y:
            cp = copy(half.at[p], got_y.at[y], y_send.at[p], y_recv.at[y], dev(p, z, c, m))
            cp.start()
            sent.append(cp)
    total = half[y]
    for p in y_peers:
        copy(half.at[p], got_y.at[p], y_send.at[p], y_recv.at[p], dev(p, z, c, m)).wait_recv()
        total = total + got_y[p]
    quarter[...] = total
    for p in z_peers:
        cp = copy(quarter.at[p], got_z.at[z], z_send.at[p], z_recv.at[z], dev(y, p, c, m))
        cp.start()
        sent.append(cp)
    row = quarter[z]
    for p in reversed(z_peers):
        copy(quarter.at[p], got_z.at[p], z_send.at[p], z_recv.at[p], dev(y, p, c, m)).wait_recv()
        row = row + got_z[p]
    mom[m, c, y, z] = row
    for p in z_peers:
        cp = copy(mom.at[m, c, y, z], mom.at[m, c, y, z], gz_send.at[p], gz_recv.at[z],
                  dev(y, p, c, m))
        cp.start()
        sent.append(cp)

    for yy, co in plane:
        cp = copy(send_rows.at[yy, :, co], between.at[y, c], d_send.at[yy * NC + co],
                  d_recv.at[y * NC + c], dev(yy, z, co, m))
        cp.start()
        sent.append(cp)
    for p in reversed(z_peers):
        copy(mom.at[m, c, y, p], mom.at[m, c, y, p], gz_send.at[p], gz_recv.at[p],
             dev(y, p, c, m)).wait_recv()
    for yy, co in plane:
        copy(send_rows.at[yy, :, co], between.at[yy, co], d_send.at[yy * NC + co],
             d_recv.at[yy * NC + co], dev(yy, z, co, m)).wait_recv()
    late = []
    for p in z_peers:
        cp = copy(between.at[:, :, p], got.at[m, :, :, z], e_send.at[p], e_recv.at[z],
                  dev(y, p, c, m))
        cp.start()
        late.append(cp)
    got[m, :, :, z] = between[:, :, z]
    lo, hi = pl.ds(0, NZ // 2), pl.ds(NZ // 2, NZ // 2)

    def piece(n, core):
        kind, peer = divmod(n + 2, 3)
        return (mom.at[m, core, y],
                mom.at[m, core, y_peers[peer], lo],
                mom.at[x_peers[peer], core, y, hi],
                mom.at[x_peers[peer], core, :, lo],
                mom.at[:, core, y_peers[peer], hi])[kind]

    def pass_on(n):
        cp = copy(piece(n, c), piece(n, c), gc_send.at[n], gc_recv.at[n], sibling)
        cp.start()
        sent.append(cp)

    for p in y_peers:
        cp = copy(mom.at[m, c, y, lo], mom.at[m, c, y, lo], a_send.at[p], a_recv.at[y],
                  dev(p, z, c, m))
        cp.start()
        sent.append(cp)
    for p in x_peers:
        cp = copy(mom.at[m, c, y, hi], mom.at[m, c, y, hi], b_send.at[p], b_recv.at[m],
                  dev(y, z, c, p))
        cp.start()
        sent.append(cp)

    def low_piece(q):
        for p in x_peers:
            cp = copy(mom.at[m, c, q, lo], mom.at[m, c, q, lo], a2_send.at[p * NY + q],
                      a2_recv.at[m * NY + q], dev(y, z, c, p))
            cp.start()
            sent.append(cp)

    def high_piece(q):
        for p in y_peers:
            cp = copy(mom.at[q, c, y, hi], mom.at[q, c, y, hi], b2_send.at[p * NX + q],
                      b2_recv.at[y * NX + q], dev(p, z, c, m))
            cp.start()
            sent.append(cp)

    low_piece(y)
    high_piece(m)
    pass_on(0)
    for n in (1, 2, 0):
        p = y_peers[n]
        copy(mom.at[m, c, p, lo], mom.at[m, c, p, lo], a_send.at[p], a_recv.at[p],
             dev(p, z, c, m)).wait_recv()
        low_piece(p)
        pass_on(1 + n)
        p = x_peers[n]
        copy(mom.at[p, c, y, hi], mom.at[p, c, y, hi], b_send.at[p], b_recv.at[p],
             dev(y, z, c, p)).wait_recv()
        high_piece(p)
        pass_on(4 + n)
    for n in (1, 2, 0):
        p = x_peers[n]
        for q in range(NY):
            copy(mom.at[p, c, q, lo], mom.at[p, c, q, lo], a2_send.at[p * NY + q],
                 a2_recv.at[p * NY + q], dev(y, z, c, p)).wait_recv()
        pass_on(7 + n)
        p = y_peers[n]
        for q in range(NX):
            copy(mom.at[q, c, p, hi], mom.at[q, c, p, hi], b2_send.at[p * NX + q],
                 b2_recv.at[p * NX + q], dev(p, z, c, m)).wait_recv()
        pass_on(10 + n)
    for n in range(13):
        copy(piece(n, 1 - c), piece(n, 1 - c), gc_send.at[n], gc_recv.at[n], sibling).wait_recv()
    for cp in sent:
        cp.wait_send()

    for i in range(0, NB, 2):
        white[i * BLK:(i + 1) * BLK, (i + 1) * BLK:(i + 2) * BLK] = jnp.zeros((BLK, BLK), bf16)
    scale = 1.0 / row_total
    eye = jnp.where(lax.broadcasted_iota(jnp.int32, (BLK, BLK), 0)
                    == lax.broadcasted_iota(jnp.int32, (BLK, BLK), 1), 0.001, 0.0)

    def at(i, j):
        return (slice(i * BLK, (i + 1) * BLK), slice(j * BLK, (j + 1) * BLK))

    def moment_block(g, i):
        return flat[pl.ds(g * N_DP * 8 + i, N_DP, stride=8), :] * scale

    @pl.loop(0, NX * N_DP // 16)
    def _(b):
        for r in range(16):
            flat[pl.ds(pl.multiple_of(b * BLK, BLK) + 8 * r, NB), :] = (
                mom[lax.div(b, 8), lax.div(lax.rem(b, 8), 4), lax.rem(b, 4), r])

    for i in range(NB):
        for g in range(4):
            j = i + g
            if j < NB:
                val = moment_block(g, i)
                work[at(i, j)] = val + eye if g == 0 else val
            elif g < 3:
                work[at(j - NB, i)] = moment_block(g, i).T

    labels = []
    following, previous, opposite = (lax.rem(m + o, NX) for o in (1, 3, 2))
    halves = (pl.ds(0, NY // 2), pl.ds(NY // 2, NY // 2))
    corner = work[at(0, 0)]
    for kk in range(NB):
        if kk == GATHER_AT:
            for p in z_peers:
                copy(between.at[:, :, p], got.at[m, :, :, p], e_send.at[p], e_recv.at[p],
                     dev(y, p, c, m)).wait_recv()
            for p in (following, previous):
                cp = copy(got.at[m], got.at[m], x_send.at[p], x_recv.at[m], (d, p))
                cp.start()
                late.append(cp)
        if kk == RELAY_AT:
            for p in (following, previous):
                copy(got.at[p], got.at[p], x_send.at[p], x_recv.at[p], (d, p)).wait_recv()
            for n, (source, p) in enumerate(((previous, following), (following, previous))):
                part_of = got.at[source, halves[n]]
                cp = copy(part_of, part_of, f_send.at[n], f_recv.at[n], (d, p))
                cp.start()
                late.append(cp)
        if kk == NB - 1:
            for n, p in enumerate((previous, following)):
                part_of = got.at[opposite, halves[n]]
                copy(part_of, part_of, f_send.at[n], f_recv.at[n], (d, p)).wait_recv()
            for k in range(PAIR):
                stage[...] = got[k].astype(f32).reshape(N_DP * (NB + 2), BLK)
                for i in range(NB):
                    rows[k * N_DP:(k + 1) * N_DP, i * BLK:(i + 1) * BLK] = (
                        stage[pl.ds(i, N_DP, stride=NB + 2), :].astype(bf16))
                labels.append(stage[pl.ds(NB, N_DP, stride=NB + 2), :])
        inverse = jnp.concatenate(
            lower_inverse([corner[8 * t:8 * t + 8, :] for t in range(BLK // 8)]), axis=0)
        rk = slice(kk * BLK, (kk + 1) * BLK)
        line = mm(stack_left(inverse, 1), stack_right(work[rk, :], 0))
        white[at(kk, kk)] = inverse.astype(bf16)
        if kk:
            white[rk, :kk * BLK] = line[:, :kk * BLK].astype(bf16)
        if kk == NB - 1:
            break
        done = (kk + 1) * BLK
        left[done:, :] = stack_left(line[:, done:].T, 1)
        right[:, done:] = stack_right(line[:, done:], 0)
        nxt = at(kk + 1, kk + 1)
        corner = work[nxt] - mm(left[nxt[0], :], right[:, nxt[1]])
        right[:, :done] = stack_right(
            jnp.concatenate([line[:, :kk * BLK], inverse], axis=1) if kk else inverse, 0)
        old = mm(left[done:, :], right[:, :done])
        if kk:
            work[done:, :kk * BLK] = work[done:, :kk * BLK] - old[:, :kk * BLK]
        work[done:, rk] = -old[:, rk]
        for i in range(kk + 1, NB, 2):
            ri = slice(i * BLK, min(i + 2, NB) * BLK)
            work[ri, i * BLK:] = work[ri, i * BLK:] - mm(left[ri, :], right[:, i * BLK:])

    for cp in late:
        cp.wait_send()
    wide = 2 * BLK
    whitened = jnp.concatenate(
        [lax.dot_general(rows[:, :n + wide], white[n:n + wide, :n + wide],
                         (((1,), (1,)), ((), ())), preferred_element_type=f32)
         for n in range(0, D, wide)], axis=1).astype(bf16)
    widened = whitened.astype(f32)
    square_sum = jnp.sum(widened * widened, axis=1, keepdims=True)
    rows[...] = (widened * lax.rsqrt(square_sum + 1e-06)).astype(bf16)
    lane = lax.broadcasted_iota(jnp.int32, (N_DP, N_DP), 1)
    other = lax.broadcasted_iota(jnp.int32, (N_DP, N_DP), 0) != lane
    flipped = [value.T for value in labels]
    reply = jnp.zeros((N_DP, N_DP), f32)
    for a in range(PAIR):
        sim = lax.dot_general(rows[a * N_DP:(a + 1) * N_DP, :], rows[...],
                              (((1,), (1,)), ((), ())), preferred_element_type=f32)
        best = jnp.full((N_DP, N_DP), -1.0, f32)
        for b in range(PAIR):
            same = (labels[a] == flipped[b]) & (labels[a] >= 0.0)
            if a == b:
                same = same & other
            best = jnp.maximum(best, jnp.where(same, sim[:, b * N_DP:(b + 1) * N_DP], -1.0))
        reply = jnp.where(lane == a, jnp.max(best, axis=1, keepdims=True), reply)
    ret[:, :, :, 0, :] = reply.reshape(NY, NC, NZ, BLK)
    back = []
    for p in z_peers:
        cp = copy(ret.at[:, :, p], ret_between.at[z], r_send.at[p], r_recv.at[z], dev(y, p, c, m))
        cp.start()
        back.append(cp)
    ret_between[z] = ret[:, :, z]
    for p in reversed(z_peers):
        copy(ret.at[:, :, p], ret_between.at[p], r_send.at[p], r_recv.at[p],
             dev(y, p, c, m)).wait_recv()
    for yy, co in plane:
        cp = copy(ret_between.at[:, yy, co], ret_got.at[y, c], t_send.at[yy * NC + co],
                  t_recv.at[y * NC + c], dev(yy, z, co, m))
        cp.start()
        back.append(cp)
    ret_got[y, c] = ret_between[:, y, c]
    spot = lax.broadcasted_iota(jnp.int32, (N_DP, count), 0)
    spot_z, spot_yc = lax.rem(spot, NZ), lax.div(spot, NZ)
    spot = (lax.div(spot_yc, NC) * NZ + spot_z) * NC + lax.rem(spot_yc, NC)
    hit = jnp.where(spot.astype(f32) == owner, 1.0, 0.0)
    for yy, co in plane:
        copy(ret_between.at[:, yy, co], ret_got.at[yy, co], t_send.at[yy * NC + co],
             t_recv.at[yy * NC + co], dev(yy, z, co, m)).wait_recv()
    for cp in back:
        cp.wait_send()
    table = lax.dot_general(ret_got[:, :, :, 0, :].reshape(N_DP, BLK), hit,
                            (((0,), (0,)), ((), ())), precision=HIGH, preferred_element_type=f32)
    score = jnp.zeros((1, count), f32)
    for k in range(PAIR):
        score = jnp.where(rank == float(k), table[k:k + 1, :], score)
    out_ref[...] = score


def local(embeddings, cluster_ids):
    row_count, feat_width = embeddings.shape
    dp_count = lax.axis_size("dp")
    f32, bf16 = jnp.float32, jnp.bfloat16
    dma = pltpu.SemaphoreType.DMA
    scratch = [
        pltpu.VMEM((NC, NY, NZ, NB, BLK), f32),
        pltpu.VMEM((NY, NZ, NB, BLK), f32),
        pltpu.VMEM((NY, NZ, NB, BLK), f32),
        pltpu.VMEM((NY, NZ, NB, BLK), f32),
        pltpu.VMEM((NZ, NB, BLK), f32),
        pltpu.VMEM((NZ, NB, BLK), f32),
        pltpu.VMEM((NX, NC, NY, NZ, NB, BLK), f32),
        pltpu.VMEM((NX * N_DP * 8, BLK), f32),
        pltpu.VMEM((N_DP * (NB + 2), BLK), f32),
        pltpu.VMEM((NY, NZ, NC, NB + 2, BLK), bf16),
        pltpu.VMEM((NY, NC, NZ, NB + 2, BLK), bf16),
        pltpu.VMEM((NX, NY, NC, NZ, NB + 2, BLK), bf16),
        pltpu.VMEM((D, D), f32),
        pltpu.VMEM((D, 6 * BLK), bf16),
        pltpu.VMEM((6 * BLK, D), bf16),
        pltpu.VMEM((D, D), bf16),
        pltpu.VMEM((PAIR * N_DP, D), bf16),
        pltpu.VMEM((NY, NC, NZ, 1, BLK), f32),
        pltpu.VMEM((NZ, NY, NC, 1, BLK), f32),
        pltpu.VMEM((NY, NC, NZ, 1, BLK), f32),
        dma((NY,)), dma((NY,)), dma((NY,)), dma((NY,)), dma((NZ,)), dma((NZ,)),
        dma((NZ,)), dma((NZ,)), dma((NY,)), dma((NY,)), dma((NX,)), dma((NX,)),
        dma((NX * NY,)), dma((NX * NY,)), dma((NX * NY,)), dma((NX * NY,)),
        dma((13,)), dma((13,)),
        dma((NY * NC,)), dma((NY * NC,)), dma((NZ,)), dma((NZ,)), dma((NX,)), dma((NX,)), dma((2,)), dma((2,)),
        dma((NZ,)), dma((NZ,)), dma((NY * NC,)), dma((NY * NC,)),
    ]
    vm = pl.BlockSpec(memory_space=pltpu.VMEM)
    scores = pl.pallas_call(
        functools.partial(kernel, float(row_count * dp_count)),
        out_shape=jax.ShapeDtypeStruct((1, row_count), f32),
        in_specs=[vm, vm],
        out_specs=vm,
        scratch_shapes=scratch,
        name="dedup",
        compiler_params=pltpu.CompilerParams(collective_id=0, has_side_effects=True),
    )(embeddings, cluster_ids.reshape(1, row_count))
    return scores.reshape(row_count)


def solution(mesh):
    in_specs = (P("dp", None), P("dp"))
    out_specs = P("dp")
    return jax.shard_map(local, mesh=mesh, in_specs=in_specs, out_specs=out_specs, check_vma=False)
```
